512 devices in a mesh: seq: 128 (over x, z, core), head: 4 (over y).
Axes of the slice: x: 4, y: 4, z: 16, core: 2. Of those that a mesh axis runs over, the one named last changes fastest.
Arguments:
- tokens: bfloat16 [128, 128, 2048], P('seq'), may hold values from -6 to 6
- attn_gain: bfloat16 [2048], replicated, may hold values from 0.099609375 to 1.8984375
- q_gain: bfloat16 [64], replicated, may hold values from 0.099609375 to 1.8984375
- k_gain: bfloat16 [64], replicated, may hold values from 0.099609375 to 1.8984375
- ffn_gain: bfloat16 [2048], replicated, may hold values from 0.099609375 to 1.8984375
- w_query: bfloat16 [2048, 1280], P('seq', 'head'), may hold values from -0.125 to 0.125
- w_keyval: bfloat16 [2048, 640], P('seq'), may hold values from -0.125 to 0.125
- w_out: bfloat16 [1280, 2048], P('head', 'seq'), may hold values from -0.15625 to 0.15625
- prior_cache: bfloat16 [128, 512, 640], P(None, 'seq')
- prior_len: int32 [128], replicated, may hold values from 0 to 512, as said below
- stretch_len: int32 [128], replicated, may hold values from 1 to 128, as said below
Outputs:
- hidden: bfloat16 [128, 128, 2048], P('seq', 'head')
- ffn_input: bfloat16 [128, 128, 2048], P('seq', 'head')
- new_cache: bfloat16 [128, 128, 640], P('seq', 'head')
- decode_cache: bfloat16 [128, 512, 640], P('seq', 'head')
The draws below stay inside these ranges and needn't reach their ends.
Inputs may be any that keep to these rules, and one draw needn't show every extreme that they name: `prior_len`: some request has all 512 slots in use. `stretch_len`: some request fills its stretch.
All inputs are finite; a program needn't handle non-finite values.
Results may differ from the reference program's by a relative error of at most 0.011.
The reference program's roundings to bfloat16 on the way count: a program that leaves them out, or rounds other values in their place, can miss the bound.
Values may be sent and summed in bfloat16 or wider, within the bound.
A program may use at most 64 MiB of HBM per device.

```python
import math
import jax
import jax.numpy as jnp
from jax import lax

D = 2048
HD = 64
QH = 20
KVH = 5
NEW = 128
REQS = 128
PRIOR = 512


def draw_prior_len(key, part):
    counts = jax.random.randint(key, (REQS,), 0, PRIOR + 1)
    chosen = jax.random.randint(jax.random.fold_in(key, 11), (), 0, REQS)
    return jnp.where(jnp.arange(REQS) == chosen, PRIOR, counts).astype(jnp.int32)


def draw_stretch_len(key, part):
    counts = jax.random.randint(key, (REQS,), 1, NEW + 1)
    chosen = jax.random.randint(jax.random.fold_in(key, 13), (), 0, REQS)
    return jnp.where(jnp.arange(REQS) == chosen, NEW, counts).astype(jnp.int32)


def draw_prior_cache(key, part):
    first = jax.random.fold_in(key, 17)
    base = jax.random.normal(first, (REQS, PRIOR, 2 * KVH * HD), jnp.float32)
    return base.astype(jnp.bfloat16)


def shard_levels(key, shape, cuts, least, largest):
    factor_of, own = 1.0, jax.random.fold_in(key, 6)
    for axis_at, shards_of in cuts:
        steps = jnp.exp(jax.random.uniform(jax.random.fold_in(own, axis_at), (shards_of,), jnp.float32, least / len(cuts), largest / len(cuts)))
        factor_of = factor_of * jnp.repeat(steps, shape[axis_at] // shards_of).reshape([-1 if axis == axis_at else 1 for axis in range(len(shape))])
    return factor_of


def noise(own_key, extent, width, limit, cuts=(), held_as=jnp.bfloat16):
    drawn = width * jax.random.normal(own_key, extent, jnp.float32)
    if cuts:
        drawn = drawn * shard_levels(own_key, extent, cuts, -0.22, 0.18)
    return jnp.clip(drawn, -limit, limit).astype(held_as)


def setup_inputs(seed: int = 0) -> dict:
    keys = jax.random.split(jax.random.key(seed), 12)
    tokens = noise(keys[0], (REQS, NEW, D), 1.0, 6.0, ((0, 128),))
    attn_gain = jnp.clip(1.0 + 0.18 * jax.random.normal(keys[1], (D,), jnp.float32), 0.099609375, 1.8984375).astype(jnp.bfloat16)
    q_gain = jnp.clip(1.0 + 0.18 * jax.random.normal(keys[2], (HD,), jnp.float32), 0.099609375, 1.8984375).astype(jnp.bfloat16)
    k_gain = jnp.clip(1.0 + 0.18 * jax.random.normal(keys[3], (HD,), jnp.float32), 0.099609375, 1.8984375).astype(jnp.bfloat16)
    ffn_gain = jnp.clip(1.0 + 0.18 * jax.random.normal(keys[4], (D,), jnp.float32), 0.099609375, 1.8984375).astype(jnp.bfloat16)
    w_query = noise(keys[5], (D, QH * HD), D ** -0.5, 0.125, ((0, 128), (1, 4)))
    w_keyval = noise(keys[6], (D, 2 * KVH * HD), D ** -0.5, 0.125, ((0, 128),))
    w_out = noise(keys[7], (QH * HD, D), (QH * HD) ** -0.5, 0.15625, ((0, 4), (1, 128)))
    prior_cache = draw_prior_cache(jax.random.fold_in(keys[11], 71), 0)
    prior_len = draw_prior_len(jax.random.fold_in(keys[11], 71), 0)
    stretch_len = draw_stretch_len(jax.random.fold_in(keys[11], 71), 0)
    return dict(tokens=tokens, attn_gain=attn_gain, q_gain=q_gain, k_gain=k_gain, ffn_gain=ffn_gain, w_query=w_query, w_keyval=w_keyval, w_out=w_out, prior_cache=prior_cache, prior_len=prior_len, stretch_len=stretch_len)


epsilon = 1e-06

def rms_norm(values, gain):
    return values * lax.rsqrt(lax.optimization_barrier(jnp.mean(values * values, axis=-1, keepdims=True)) + epsilon) * gain

def rotary(values, positions):
    middle = values.shape[-1] // 2
    inverse = jnp.exp(jnp.arange(middle, dtype=jnp.float32) * (-2.0 * math.log(10000.0) / values.shape[-1]))
    angles = positions.astype(jnp.float32)[:, None] * inverse[None, :]
    cosine = jnp.concatenate([jnp.cos(angles), jnp.cos(angles)], axis=-1)[:, None, :]
    sine = jnp.concatenate([jnp.sin(angles), jnp.sin(angles)], axis=-1)[:, None, :]
    turned = jnp.concatenate([-values[..., middle:], values[..., :middle]], axis=-1)
    return values * cosine + turned * sine

def reference(tokens, attn_gain, q_gain, k_gain, ffn_gain, w_query, w_keyval, w_out, prior_cache, prior_len, stretch_len):
    width_kv = KVH * HD
    score_scale = 1.0 / math.sqrt(HD)
    group = jnp.arange(QH, dtype=jnp.int32) // (QH // KVH)
    offsets = jnp.arange(NEW, dtype=jnp.int32)
    causal = offsets[None, :] <= offsets[:, None]

    def one_request(packed):
        token_rows, stored, prior_count, stretch_count = packed
        source = token_rows.astype(jnp.float32)
        normed = rms_norm(source, attn_gain.astype(jnp.float32)).astype(jnp.bfloat16)
        query = jnp.dot(normed, w_query, preferred_element_type=jnp.float32).reshape(NEW, QH, HD)
        keyval = jnp.dot(normed, w_keyval, preferred_element_type=jnp.float32)
        positions = prior_count + offsets
        query = rotary(rms_norm(query, q_gain.astype(jnp.float32)), positions).astype(jnp.bfloat16)
        fresh_keys = rotary(rms_norm(keyval[:, :width_kv].reshape(NEW, KVH, HD), k_gain.astype(jnp.float32)), positions).astype(jnp.bfloat16)
        fresh_values = keyval[:, width_kv:].reshape(NEW, KVH, HD).astype(jnp.bfloat16)
        valid = offsets < stretch_count
        fresh = jnp.concatenate([fresh_keys.reshape(NEW, width_kv), fresh_values.reshape(NEW, width_kv)], axis=1)
        fresh = jnp.where(valid[:, None], fresh, jnp.zeros_like(fresh))
        all_keys = jnp.concatenate([stored[:, :width_kv].reshape(PRIOR, KVH, HD), fresh_keys], axis=0)
        all_values = jnp.concatenate([stored[:, width_kv:].reshape(PRIOR, KVH, HD), fresh_values], axis=0)
        key_heads = jnp.take(all_keys, group, axis=1).astype(jnp.float32)
        value_heads = jnp.take(all_values, group, axis=1).astype(jnp.float32)
        scores = jnp.einsum('qhd,khd->hqk', query.astype(jnp.float32), key_heads) * score_scale
        earlier = jnp.arange(PRIOR, dtype=jnp.int32)[None, :] < prior_count
        allowed = jnp.concatenate([jnp.broadcast_to(earlier, (NEW, PRIOR)), causal], axis=1)
        scores = jnp.where(allowed[None], scores, -jnp.inf)
        top = lax.optimization_barrier(jnp.max(scores, axis=-1, keepdims=True))
        weights = jnp.exp(scores - top)
        total = lax.optimization_barrier(jnp.sum(weights, axis=-1))
        rounded = lax.optimization_barrier(weights.astype(jnp.bfloat16)).astype(jnp.float32)
        mixed = jnp.einsum('hqk,khd->qhd', rounded, value_heads) / total.T[:, :, None]
        attended = mixed.astype(jnp.bfloat16).reshape(NEW, QH * HD)
        residual = source + jnp.dot(attended, w_out, preferred_element_type=jnp.float32)
        hidden = jnp.where(valid[:, None], residual, 0.0).astype(jnp.bfloat16)
        ffn_input = jnp.where(valid[:, None], rms_norm(residual, ffn_gain.astype(jnp.float32)), 0.0).astype(jnp.bfloat16)
        return (hidden, ffn_input, fresh)
    hidden, ffn_input, new_cache = lax.map(one_request, (tokens, prior_cache, prior_len, stretch_len))
    return (hidden, ffn_input, new_cache, prior_cache)
```

```python
import math

import jax
import jax.numpy as jnp
from jax import lax
from jax.experimental import pallas as pl
from jax.experimental.pallas import tpu as pltpu
from jax.sharding import PartitionSpec as P

HD = 64
QH = 20
KVH = 5
NX, NZ, NY = 4, 16, 4
PLANE = NZ * 2
WIDE = 896
MESH = pl.DeviceIdType.MESH

epsilon = 1e-06


def rms_norm(values, gain):
    return values * lax.rsqrt(jnp.mean(values * values, axis=-1, keepdims=True) + epsilon) * gain


def rotary(values, positions):
    middle = values.shape[-1] // 2
    inverse = jnp.exp(
        jnp.arange(middle, dtype=jnp.float32) * (-2.0 * math.log(10000.0) / values.shape[-1])
    )
    angles = positions.astype(jnp.float32)[:, None] * inverse[None, :]
    cosine = jnp.concatenate([jnp.cos(angles), jnp.cos(angles)], axis=-1)[:, None, :]
    sine = jnp.concatenate([jnp.sin(angles), jnp.sin(angles)], axis=-1)[:, None, :]
    turned = jnp.concatenate([-values[..., middle:], values[..., :middle]], axis=-1)
    return values * cosine + turned * sine


def tile_of(head, j):
    first = jnp.where(head >= 2, 1, 0)
    second = jnp.where(head == 0, 2, jnp.where(head == 1, 1, jnp.where(head == 2, 3, 2)))
    third = jnp.where(head >= 2, 4, 3)
    return (first, second, third)[j]


def gather_kernel(
    pack_ref, cache_ref, w_ref, d_ref, e_ref, x_buf, w_send, w_recv, x_send, x_recv, d_send, d_recv, e_send, e_recv
):
    s = lax.axis_index("seq")
    h = lax.axis_index("head")
    x = s // PLANE
    low = lax.rem(s, PLANE)
    z = low // 2
    c = lax.rem(low, 2)

    def sid(xx, zz, cc):
        return xx * PLANE + zz * 2 + cc

    def wrapx(v):
        return lax.rem(v + NX, NX)

    def wrapz(v):
        return lax.rem(v + NZ, NZ)

    barrier = pltpu.get_barrier_semaphore()

    def greet(k, carry):
        pl.semaphore_signal(
            barrier, inc=1, device_id={"seq": x * PLANE + lax.rem(low + k, PLANE)}, device_id_type=MESH
        )
        return carry

    lax.fori_loop(1, PLANE, greet, 0)
    for k in range(1, NX):
        pl.semaphore_signal(
            barrier, inc=1, device_id={"seq": sid(wrapx(x + k), z, c)}, device_id_type=MESH
        )
    for k in range(1, NY):
        pl.semaphore_signal(
            barrier, inc=1, device_id={"head": lax.rem(h + k, NY)}, device_id_type=MESH
        )
    pl.semaphore_wait(barrier, PLANE - 1 + NX - 1 + NY - 1)

    mine = cache_ref.at[pl.ds(pl.multiple_of(x * PLANE, PLANE), PLANE)]

    @pl.when(x == h)
    def _():
        for k in range(1, NX):
            xx = wrapx(x + k)
            pltpu.make_async_remote_copy(
                src_ref=cache_ref.at[pl.ds(pl.multiple_of(xx * PLANE, PLANE), PLANE)],
                dst_ref=x_buf,
                send_sem=x_send.at[k - 1],
                recv_sem=x_recv,
                device_id={"seq": sid(xx, z, c)},
                device_id_type=MESH,
            ).start()
        pltpu.make_async_copy(mine, x_buf, x_recv).start()

    ahead = jnp.where(c == 0, 1, -1)
    partner = {"seq": sid(x, z, 1 - c)}

    def rows(b):
        return w_ref.at[pl.ds(pl.multiple_of(b * 16, 16), 16)]

    def push(b, target, src=None):
        pltpu.make_async_remote_copy(
            src_ref=rows(b) if src is None else src,
            dst_ref=rows(b),
            send_sem=w_send,
            recv_sem=w_recv.at[b],
            device_id=target,
            device_id_type=MESH,
        ).start()

    def arrive(b):
        pltpu.make_async_copy(rows(b), rows(b), w_recv.at[b]).wait()

    along = {"seq": sid(wrapx(x + ahead), z, c)}
    against = {"seq": sid(wrapx(x - ahead), z, c)}
    up = {"seq": sid(x, wrapz(z + 1), c)}
    down = {"seq": sid(x, wrapz(z - 1), c)}

    pltpu.make_async_copy(pack_ref, rows(s), w_recv.at[s]).start()
    push(s, up, pack_ref)
    push(s, down, pack_ref)
    push(s, along, pack_ref)
    push(s, against, pack_ref)
    push(s, partner, pack_ref)

    def spread(b):
        push(b, along)
        push(b, against)
        push(b, partner)

    def relay(zb):
        b = sid(wrapx(x - ahead), zb, c)
        arrive(b)
        push(b, along)
        push(b, partner)
        b = sid(wrapx(x + ahead), zb, c)
        arrive(b)
        push(b, partner)

    def last(zb):
        b = sid(wrapx(x + 2), zb, c)
        arrive(b)
        push(b, partner)

    HALF = NZ // 2
    for t in range(1, HALF + 1):
        b = sid(x, wrapz(z - t), c)
        arrive(b)
        if t < HALF:
            push(b, up)
        spread(b)
        if t < HALF:
            b = sid(x, wrapz(z + t), c)
            arrive(b)
            if t < HALF - 1:
                push(b, down)
            spread(b)
        if t == 2:
            pltpu.make_async_copy(x_buf, x_buf, x_recv).wait()

            def hand(k, carry):
                to = lax.rem(low + k, PLANE)
                pltpu.make_async_remote_copy(
                    src_ref=x_buf.at[to],
                    dst_ref=d_ref.at[low],
                    send_sem=d_send,
                    recv_sem=d_recv,
                    device_id={"seq": x * PLANE + to},
                    device_id_type=MESH,
                ).start()
                return carry

            lax.fori_loop(1, PLANE, hand, 0)
            pltpu.make_async_copy(x_buf.at[low], d_ref.at[low], d_recv).start()
        u = t - 2
        if u == 0:
            relay(z)
        if 0 < u < HALF:
            relay(wrapz(z - u))
            relay(wrapz(z + u))
        u = t - 4
        if u == 0:
            last(z)
        if 0 < u < HALF:
            last(wrapz(z - u))
            last(wrapz(z + u))
    pltpu.make_async_copy(d_ref, d_ref, d_recv).wait()
    for k in range(1, NY):
        to = lax.rem(h + k, NY)
        for j in range(3):
            pltpu.make_async_remote_copy(
                src_ref=d_ref.at[:, :, pl.ds(pl.multiple_of(tile_of(to, j) * 128, 128), 128)],
                dst_ref=e_ref.at[h, j],
                send_sem=e_send,
                recv_sem=e_recv,
                device_id={"head": to},
                device_id_type=MESH,
            ).start()
    for j in range(3):
        pltpu.make_async_copy(
            d_ref.at[:, :, pl.ds(pl.multiple_of(tile_of(h, j) * 128, 128), 128)], e_ref.at[h, j], e_recv
        ).start()
    relay(wrapz(z - HALF + 1))
    relay(wrapz(z + HALF - 1))
    relay(wrapz(z + HALF))
    for u in range(HALF - 3, HALF):
        last(wrapz(z - u))
        last(wrapz(z + u))
    last(wrapz(z + HALF))

    arrive(s)
    other = s + 1 - 2 * c

    def shared(k, carry):
        b = (s // 2 * 2 + 2 * k + 1 - c) % (NX * PLANE)
        arrive(b)
        return carry

    lax.fori_loop(0, NX * NZ, shared, 0)
    pltpu.make_async_copy(e_ref, e_ref, e_recv).wait()
    for k in range(NX - 1):

        @pl.when(x == h)
        def _(k=k):
            pltpu.make_async_copy(mine, mine, x_send.at[k]).wait()

    pltpu.make_async_copy(d_ref.at[pl.ds(0, PLANE - 1)], d_ref.at[pl.ds(0, PLANE - 1)], d_send).wait()
    pltpu.make_async_copy(e_ref.at[pl.ds(0, NY - 1)], e_ref.at[pl.ds(0, NY - 1)], e_send).wait()
    sent = 2 * NX * NZ - 1
    pltpu.make_async_copy(w_ref.at[pl.ds(0, sent * 16)], w_ref.at[pl.ds(0, sent * 16)], w_send).wait()


def gather(pack, cache):
    vmem = pl.BlockSpec(memory_space=pltpu.VMEM)
    return pl.pallas_call(
        gather_kernel,
        out_shape=(
            jax.ShapeDtypeStruct((2048, WIDE), jnp.bfloat16),
            jax.ShapeDtypeStruct((PLANE, 4, 640), jnp.bfloat16),
            jax.ShapeDtypeStruct((NY, 3, PLANE, 4, 128), jnp.bfloat16),
        ),
        in_specs=[vmem, pl.BlockSpec(memory_space=pl.ANY)],
        out_specs=(vmem, vmem, vmem),
        scratch_shapes=[
            pltpu.VMEM((PLANE, 4, 640), jnp.bfloat16),
            pltpu.SemaphoreType.DMA,
            pltpu.SemaphoreType.DMA((NX * PLANE,)),
            pltpu.SemaphoreType.DMA((NX - 1,)),
            pltpu.SemaphoreType.DMA,
            pltpu.SemaphoreType.DMA,
            pltpu.SemaphoreType.DMA,
            pltpu.SemaphoreType.DMA,
            pltpu.SemaphoreType.DMA,
        ],
        compiler_params=pltpu.CompilerParams(collective_id=0, has_side_effects=True),
        name="gather",
    )(pack, cache)


def swap_kernel(terms_ref, kv_ref, t_ref, k_ref, t_send, t_recv, k_send, k_recv):
    h = lax.axis_index("head")
    barrier = pltpu.get_barrier_semaphore()
    for k in range(1, NY):
        pl.semaphore_signal(
            barrier, inc=1, device_id={"head": lax.rem(h + k, NY)}, device_id_type=MESH
        )
    pl.semaphore_wait(barrier, NY - 1)
    for k in (2, 1, 3):
        to = lax.rem(h + k, NY)
        for src, dst, ss, rs in ((terms_ref, t_ref, t_send, t_recv), (kv_ref, k_ref, k_send, k_recv)):
            pltpu.make_async_remote_copy(
                src_ref=src.at[to],
                dst_ref=dst.at[h],
                send_sem=ss,
                recv_sem=rs,
                device_id={"head": to},
                device_id_type=MESH,
            ).start()
    pltpu.make_async_copy(terms_ref.at[h], t_ref.at[h], t_recv).start()
    pltpu.make_async_copy(kv_ref.at[h], k_ref.at[h], k_recv).start()
    for ref, ss, rs in ((t_ref, t_send, t_recv), (k_ref, k_send, k_recv)):
        pltpu.make_async_copy(ref, ref, rs).wait()
        part = ref.at[pl.ds(0, NY - 1)]
        pltpu.make_async_copy(part, part, ss).wait()


def swap(terms, kv):
    vmem = pl.BlockSpec(memory_space=pltpu.VMEM)
    return pl.pallas_call(
        swap_kernel,
        out_shape=(
            jax.ShapeDtypeStruct(terms.shape, terms.dtype),
            jax.ShapeDtypeStruct(kv.shape, kv.dtype),
        ),
        in_specs=[vmem, vmem],
        out_specs=(vmem, vmem),
        scratch_shapes=[pltpu.SemaphoreType.DMA] * 4,
        compiler_params=pltpu.CompilerParams(collective_id=1, has_side_effects=True),
        name="swap",
    )(terms, kv)


def half_swap(a, b):
    return jnp.concatenate([a[:, 64:], b[:, :64]], axis=1)


def shards(tokens, attn_gain, q_gain, k_gain, ffn_gain, w_query, w_keyval, w_out, prior_cache, prior_len, stretch_len):
    seq_index = lax.axis_index("seq")
    h = lax.axis_index("head")
    length = tokens.shape[1]
    score_scale = 1.0 / math.sqrt(HD)
    pack = jnp.concatenate(
        [
            lax.dynamic_slice_in_dim(w_keyval, 64 * h, 128, 1),
            lax.dynamic_slice_in_dim(w_keyval, 320 + 64 * h, 128, 1),
            w_query,
            w_out.T,
        ],
        axis=1,
    )
    weights, decode, stored = gather(pack, prior_cache)
    flat = tokens[0]
    normed = rms_norm(flat.astype(jnp.float32), attn_gain.astype(jnp.float32)).astype(jnp.bfloat16)
    first = jnp.dot(normed, weights[:, :576], preferred_element_type=jnp.float32)
    prior_count = lax.dynamic_index_in_dim(prior_len, seq_index, keepdims=False)
    stretch_count = lax.dynamic_index_in_dim(stretch_len, seq_index, keepdims=False)
    offsets = jnp.arange(length, dtype=jnp.int32)
    positions = prior_count + offsets
    query = rotary(
        rms_norm(first[:, 256:].reshape(length, 5, HD), q_gain.astype(jnp.float32)), positions
    ).astype(jnp.bfloat16)
    keys = rotary(
        rms_norm(first[:, :128].reshape(length, 2, HD), k_gain.astype(jnp.float32)), positions
    ).astype(jnp.bfloat16).reshape(length, 128)
    values = first[:, 128:256].astype(jnp.bfloat16)
    tiles = [stored[:, j].reshape(512, 128) for j in range(3)]
    even = h % 2 == 0
    k_prior = jnp.where(even, tiles[0], half_swap(tiles[0], tiles[1]))
    v_prior = jnp.where(even, half_swap(tiles[1], tiles[2]), tiles[2])
    all_keys = jnp.concatenate([k_prior, keys], axis=0)
    all_values = jnp.concatenate([v_prior, values], axis=0)
    which = (jnp.arange(5) >= 4 - h)
    lane_second = jnp.arange(128) >= 64
    spread = jnp.concatenate([query, query], axis=2)
    spread = jnp.where(which[None, :, None] == lane_second[None, None, :], spread, jnp.zeros_like(spread))
    scores = jnp.einsum("qhd,kd->hqk", spread, all_keys, preferred_element_type=jnp.float32) * score_scale
    earlier = jnp.arange(512, dtype=jnp.int32)[None, :] < prior_count
    allowed = jnp.concatenate(
        [jnp.broadcast_to(earlier, (length, 512)), offsets[None, :] <= offsets[:, None]], axis=1
    )
    scores = jnp.where(allowed[None], scores, -jnp.inf)
    top = jnp.max(scores, axis=-1, keepdims=True)
    w = jnp.exp(scores - top)
    total = jnp.sum(w, axis=-1)
    mixed = jnp.einsum("hqk,kd->qhd", w.astype(jnp.bfloat16), all_values, preferred_element_type=jnp.float32)
    mixed = jnp.where(which[None, :, None], mixed[..., 64:], mixed[..., :64]) / total.T[:, :, None]
    attended = mixed.astype(jnp.bfloat16).reshape(length, 320)
    terms = lax.dot_general(
        attended, weights[:, 576:], (((1,), (1,)), ((), ())), preferred_element_type=jnp.float32
    ).astype(jnp.bfloat16)
    got, kv = swap(terms.reshape(NY, 32, 2048), jnp.concatenate([keys, values], axis=1).reshape(NY, 32, 256))
    summed = jnp.sum(got.astype(jnp.float32), axis=0)
    own_tokens = lax.dynamic_slice_in_dim(flat, h * 32, 32, 0).astype(jnp.float32)
    residual = own_tokens + summed
    valid = (h * 32 + jnp.arange(32, dtype=jnp.int32))[:, None] < stretch_count
    hidden = jnp.where(valid, residual, 0.0).astype(jnp.bfloat16)
    ffn_input = jnp.where(valid, rms_norm(residual, ffn_gain.astype(jnp.float32)), 0.0).astype(jnp.bfloat16)
    fresh = jnp.concatenate(
        [kv[0][:, :128], kv[2][:, :128], kv[3][:, 64:128], kv[0][:, 128:192], kv[1][:, 128:], kv[3][:, 128:]], axis=1
    )
    fresh = jnp.where(valid, fresh, jnp.zeros_like(fresh))
    return (hidden[None], ffn_input[None], fresh[None], decode.reshape(1, 128, 640))


def solution(mesh):
    placed = (
        P("seq", None, None),
        P(),
        P(),
        P(),
        P(),
        P("seq", "head"),
        P("seq", None),
        P("head", "seq"),
        P(None, "seq", None),
        P(),
        P(),
    )
    return jax.shard_map(
        shards,
        mesh=mesh,
        in_specs=placed,
        out_specs=(
            P("seq", "head", None),
            P("seq", "head", None),
            P("seq", "head", None),
            P("seq", "head", None),
        ),
        check_vma=False,
    )
```

```python
import math

import jax
import jax.numpy as jnp
from jax import lax
from jax.experimental import pallas as pl
from jax.experimental.pallas import tpu as pltpu
from jax.sharding import PartitionSpec as P

HD = 64
NX, NZ, NY = 4, 16, 4
PLANE = NZ * 2
A, B = 640, 256
MESH = pl.DeviceIdType.MESH
BF = jnp.bfloat16
F32 = jnp.float32
epsilon = 1e-06


def body(
    tok, again, qgain, kgain, fgain, wq, wkv, wo, cache, cosine, sine, prior, stretch,
    hidden, ffn, fresh, decode,
    wa, wb, cpack, xb, eb, yb, normed, acc, qs, kvs, kvr, tb, rb,
    a_send, a_recv, b_send, b_recv, x_send, x_recv, e_send, e_recv, y_send, y_recv, k_send, k_recv, t_send, t_recv,
):
    s = lax.axis_index("seq")
    h = lax.axis_index("head")
    x = s // PLANE
    low = lax.rem(s, PLANE)
    z = low // 2
    c = lax.rem(low, 2)

    def sid(xx, zz, cc):
        return xx * PLANE + zz * 2 + cc

    def wrapx(v):
        return lax.rem(v + NX, NX)

    def wrapz(v):
        return lax.rem(v + NZ, NZ)

    barrier = pltpu.get_barrier_semaphore()

    def signal(target):
        pl.semaphore_signal(barrier, inc=1, device_id=target, device_id_type=MESH)

    def greet(k, carry):
        signal({"seq": x * PLANE + lax.rem(low + k, PLANE)})
        return carry

    lax.fori_loop(1, PLANE, greet, 0)
    for k in range(1, NX):
        signal({"seq": sid(wrapx(x + k), z, c)})
    for k in range(1, NY):
        signal({"head": lax.rem(h + k, NY)})

    own = pl.ds(pl.multiple_of(s * 16, 16), 16)
    for head in range(NY):

        @pl.when(h == head)
        def _(head=head):
            lo = 64 * head
            wa[own, 0:128] = wkv[:, lo : lo + 128]
            wa[own, 128:256] = wkv[:, 320 + lo : 448 + lo]

            def pack(i, carry):
                at = pl.ds(pl.multiple_of(i * 16, 16), 16)
                cpack[at, :, 0:128] = cache[at, :, lo : lo + 128]
                cpack[at, :, 128:256] = cache[at, :, 320 + lo : 448 + lo]
                return carry

            lax.fori_loop(0, 8, pack, 0)

    wa[own, 256:640] = jnp.concatenate([wq[...], wo[:, 0:64]], axis=1)
    wb[own, :] = wo[:, 64:320]

    def norm(i, carry):
        at = pl.ds(pl.multiple_of(i * 16, 16), 16)
        v = tok[at, :].astype(F32)
        v = v * lax.rsqrt(jnp.mean(v * v, axis=-1, keepdims=True) + epsilon) * again[...]
        normed[at, :] = v.astype(BF)
        return carry

    lax.fori_loop(0, 8, norm, 0)
    pl.semaphore_wait(barrier, PLANE - 1 + NX - 1 + NY - 1)

    ahead = jnp.where(c == 0, 1, -1)
    partner = {"seq": sid(x, z, 1 - c)}

    def tox(d):
        return {"seq": sid(wrapx(x + d), z, c)}

    def toz(d):
        return {"seq": sid(x, wrapz(z + d), c)}

    class Ring:
        def __init__(self, buf, send, recv):
            self.buf, self.send, self.recv, self.count = buf, send, recv, 0

        def rows(self, b):
            return self.buf.at[pl.ds(pl.multiple_of(b * 16, 16), 16)]

        def push(self, b, target):
            self.count += 1
            pltpu.make_async_remote_copy(
                src_ref=self.rows(b),
                dst_ref=self.rows(b),
                send_sem=self.send,
                recv_sem=self.recv.at[b],
                device_id=target,
                device_id_type=MESH,
            ).start()

        def arrive(self, b):
            pltpu.make_async_copy(self.rows(b), self.rows(b), self.recv.at[b]).wait()

        def spread(self, b):
            self.push(b, tox(ahead))
            self.push(b, tox(-ahead))
            self.push(b, partner)

        def near(self, b):
            for d in (2, 1, -1):
                self.push(b, toz(d))

        def start(self):
            for d in (8, 4, -4):
                self.push(s, toz(d))
            self.near(s)
            self.spread(s)

        def here(self, d, far=False):
            b = sid(x, wrapz(z + d), c)
            self.arrive(b)
            if far:
                self.near(b)
            self.spread(b)

        def relay(self, d):
            b = sid(wrapx(x - ahead), wrapz(z + d), c)
            self.arrive(b)
            self.push(b, tox(ahead))
            self.push(b, partner)
            b = sid(wrapx(x + ahead), wrapz(z + d), c)
            self.arrive(b)
            self.push(b, partner)

        def last(self, d):
            b = sid(wrapx(x + 2), wrapz(z + d), c)
            self.arrive(b)
            self.push(b, partner)

        def shared(self, xx):
            def one(zz, carry):
                self.arrive(sid(xx, zz, 1 - c))
                return carry

            lax.fori_loop(0, NZ, one, 0)

        def drain(self):
            left = self.count
            while left > 0:
                n = min(left, 128)
                part = self.buf.at[pl.ds(0, n * 16)]
                pltpu.make_async_copy(part, part, self.send).wait()
                left -= n

    ra, rbq = Ring(wa, a_send, a_recv), Ring(wb, b_send, b_recv)
    ra.start()
    for k in (2, 1, 3):
        xx = wrapx(x + k)
        pltpu.make_async_remote_copy(
            src_ref=cpack.at[pl.ds(pl.multiple_of(xx * PLANE, PLANE), PLANE)],
            dst_ref=xb.at[x],
            send_sem=x_send,
            recv_sem=x_recv,
            device_id=tox(k),
            device_id_type=MESH,
        ).start()
    pltpu.make_async_copy(cpack.at[pl.ds(pl.multiple_of(x * PLANE, PLANE), PLANE)], xb.at[x], x_recv).start()
    near, far = (-1, 1, -2), (-4, 4, 8)
    rest = (-5, -3, 3, 5, -6, 2, 7, -7, 6)
    rbq.start()
    for d in near:
        ra.here(d)
    for d in far:
        ra.here(d, True)
    pltpu.make_async_copy(xb, xb, x_recv).wait()

    def hand(k, carry):
        to = lax.rem(low + k, PLANE)
        pltpu.make_async_remote_copy(
            src_ref=xb.at[:, to],
            dst_ref=eb.at[:, low],
            send_sem=e_send,
            recv_sem=e_recv,
            device_id={"seq": x * PLANE + to},
            device_id_type=MESH,
        ).start()
        return carry

    lax.fori_loop(1, PLANE, hand, 0)
    pltpu.make_async_copy(xb.at[:, low], eb.at[:, low], e_recv).start()
    ra.relay(0)
    for d in near:
        ra.relay(d)
    ra.last(0)
    for d in rest[:4]:
        ra.here(d)
    for d in near:
        rbq.here(d)
    for d in far:
        rbq.here(d, True)
    for d in rest[4:]:
        ra.here(d)
    for d in far:
        ra.relay(d)
    for d in near:
        ra.last(d)
    for d in rest[:4]:
        ra.relay(d)
    rbq.relay(0)
    for d in near:
        rbq.relay(d)
    for d in far:
        ra.last(d)
    for d in rest[4:]:
        ra.relay(d)
    ra.shared(x)

    def project(xx, first=False):
        deep = pl.ds(pl.multiple_of(xx * 512, 512), 512)
        part = jnp.dot(normed[:, deep], wa[deep, :], preferred_element_type=F32)
        if first:
            acc[...] = part
        else:
            acc[...] += part

    project(x, True)
    for d in rest:
        ra.last(d)
    for d in rest:
        rbq.here(d)
    ra.shared(wrapx(x + 1))
    project(wrapx(x + 1))
    ra.shared(wrapx(x - 1))
    project(wrapx(x - 1))
    rbq.last(0)
    for d in far:
        rbq.relay(d)
    for d in near:
        rbq.last(d)
    ra.shared(wrapx(x + 2))
    project(wrapx(x + 2))
    for d in rest:
        rbq.relay(d)

    lane = lax.broadcasted_iota(jnp.int32, (128, 128), 1)
    row = lax.broadcasted_iota(jnp.int32, (128, 128), 0)
    upper = lane >= 64
    flip = lax.rem(lane, 64) < 32

    def position(t, gain):
        sq = t * t
        lo = jnp.sum(jnp.where(upper, 0.0, sq), axis=-1, keepdims=True)
        hi = jnp.sum(jnp.where(upper, sq, 0.0), axis=-1, keepdims=True)
        v = t * lax.rsqrt(jnp.where(upper, hi, lo) * (1.0 / 64) + epsilon) * gain
        turned = jnp.where(flip, pltpu.roll(v, 96, 1), pltpu.roll(v, 32, 1))
        return v * cosine[...] + turned * sine[...]

    keys = position(acc[:, 0:128], kgain[...]).astype(BF)
    values = acc[:, 128:256].astype(BF)
    kvs[:, :, 0:128] = keys.reshape(NY, 32, 128)
    kvs[:, :, 128:256] = values.reshape(NY, 32, 128)
    kvr[h] = kvs[h]
    for k in (2, 1, 3):
        to = lax.rem(h + k, NY)
        pltpu.make_async_remote_copy(
            src_ref=kvs.at[to],
            dst_ref=kvr.at[h],
            send_sem=k_send,
            recv_sem=k_recv,
            device_id={"head": to},
            device_id_type=MESH,
        ).start()
    second = [jnp.where(i >= 4 - h, 1, 0) for i in range(5)]
    for pair in range(3):
        t = position(acc[:, 256 + 128 * pair : 384 + 128 * pair], qgain[...])
        r = pltpu.roll(t, 64, 1)
        for half in range(2):
            i = 2 * pair + half
            if i < 5:
                v = jnp.where(second[i] == half, t, r)
                v = jnp.where(jnp.where(upper, 1, 0) == second[i], v, 0.0)
                qs[128 * i : 128 * (i + 1), :] = v.astype(BF)

    pltpu.make_async_copy(eb, eb, e_recv).wait()
    for k in (2, 1, 3):
        to = lax.rem(h + k, NY)
        pltpu.make_async_remote_copy(
            src_ref=eb.at[to],
            dst_ref=yb.at[h],
            send_sem=y_send,
            recv_sem=y_recv,
            device_id={"head": to},
            device_id_type=MESH,
        ).start()
    pltpu.make_async_copy(eb.at[h], yb.at[h], y_recv).start()
    stored = [eb[p].reshape(128, 256) for p in range(4)]
    all_keys = jnp.concatenate([t[:, 0:128] for t in stored] + [keys], axis=0)
    all_values = jnp.concatenate([t[:, 128:256] for t in stored] + [values], axis=0)
    prior_count = prior[s]
    slot = lax.broadcasted_iota(jnp.int32, (128, 512), 1)
    earlier = slot < prior_count
    causal = lane <= row
    allowed = jnp.concatenate([earlier, causal], axis=1)
    heads = []
    for i in range(5):
        sc = lax.dot_general(
            qs[128 * i : 128 * (i + 1), :], all_keys, (((1,), (1,)), ((), ())), preferred_element_type=F32
        ) * (1.0 / math.sqrt(HD))
        sc = jnp.where(allowed, sc, -jnp.inf)
        w = jnp.exp(sc - jnp.max(sc, axis=-1, keepdims=True))
        total = jnp.sum(w, axis=-1, keepdims=True)
        m = jnp.dot(w.astype(BF), all_values, preferred_element_type=F32) / total
        heads.append(jnp.where(second[i] == (i + 1) % 2, m, pltpu.roll(m, 64, 1)))
    att = [
        jnp.where(upper, heads[0], 0.0).astype(BF),
        jnp.where(upper, heads[2], heads[1]).astype(BF),
        jnp.where(upper, heads[4], heads[3]).astype(BF),
    ]
    att12 = jnp.concatenate(att[1:], axis=1)

    def project_out(xx):
        wide = pl.ds(pl.multiple_of(xx * 512, 512), 512)
        dims = (((1,), (1,)), ((), ()))
        part = lax.dot_general(att[0], wa[wide, 512:640], dims, preferred_element_type=F32)
        part = part + lax.dot_general(att12, wb[wide, :], dims, preferred_element_type=F32)
        tb[:, :, wide] = part.astype(BF).reshape(NY, 32, 512)
        for k in (2, 1, 3):
            to = lax.rem(h + k, NY)
            pltpu.make_async_remote_copy(
                src_ref=tb.at[to, :, wide],
                dst_ref=rb.at[h, :, wide],
                send_sem=t_send,
                recv_sem=t_recv,
                device_id={"head": to},
                device_id_type=MESH,
            ).start()

    rbq.shared(x)
    project_out(x)
    for d in far + rest:
        rbq.last(d)
    for d in (1, -1, 2):
        rbq.shared(wrapx(x + d))
        project_out(wrapx(x + d))

    limit = stretch[s]

    def assemble(t0, t1, t2, t3):
        low_half = lax.broadcasted_iota(jnp.int32, (t0.shape[0], 128), 1) < 64
        mid = pltpu.roll(jnp.where(low_half, t0[:, 128:256].astype(F32), t3[:, 0:128].astype(F32)), 64, 1).astype(BF)
        return jnp.concatenate([t0[:, 0:128], t2[:, 0:128], mid, t1[:, 128:256], t3[:, 128:256]], axis=1)

    pltpu.make_async_copy(yb, yb, y_recv).wait()
    decode[...] = assemble(*[yb[p].reshape(128, 256) for p in range(4)])
    three = kvr.at[pl.ds(0, 3)]
    pltpu.make_async_copy(three, three, k_recv).wait()
    rows = h * 32 + lax.broadcasted_iota(jnp.int32, (32, 640), 0)
    made = assemble(*[kvr[p] for p in range(4)])
    fresh[...] = jnp.where(rows < limit, made, jnp.zeros_like(made))

    three = rb.at[pl.ds(0, 3)]
    pltpu.make_async_copy(three, three, t_recv).wait()
    summed = tok[pl.ds(pl.multiple_of(h * 32, 32), 32), :].astype(F32)
    share = tb[h].astype(F32)
    for k in range(1, NY):
        share = share + rb[lax.rem(h + k, NY)].astype(F32)
    resid = summed + share
    valid = h * 32 + lax.broadcasted_iota(jnp.int32, (32, 2048), 0) < limit
    hidden[...] = jnp.where(valid, resid, 0.0).astype(BF)
    scaled = resid * lax.rsqrt(jnp.mean(resid * resid, axis=-1, keepdims=True) + epsilon) * fgain[...]
    ffn[...] = jnp.where(valid, scaled, 0.0).astype(BF)

    for ref, sem in ((xb.at[pl.ds(0, 3)], x_send), (eb.at[:, pl.ds(0, PLANE - 1)], e_send),
                     (yb.at[pl.ds(0, 3)], y_send), (kvr.at[pl.ds(0, 3)], k_send), (rb.at[pl.ds(0, 3)], t_send)):
        pltpu.make_async_copy(ref, ref, sem).wait()
    ra.drain()
    rbq.drain()


def block(*args):
    vmem = pl.BlockSpec(memory_space=pltpu.VMEM)
    smem = pl.BlockSpec(memory_space=pltpu.SMEM)
    dma = pltpu.SemaphoreType.DMA
    many = pltpu.SemaphoreType.DMA((NX * PLANE,))
    cache_like = pltpu.VMEM((NX, PLANE, 4, 256), BF)
    return pl.pallas_call(
        body,
        out_shape=(
            jax.ShapeDtypeStruct((32, 2048), BF),
            jax.ShapeDtypeStruct((32, 2048), BF),
            jax.ShapeDtypeStruct((32, 640), BF),
            jax.ShapeDtypeStruct((128, 640), BF),
        ),
        in_specs=[vmem] * 11 + [smem] * 2,
        out_specs=(vmem,) * 4,
        scratch_shapes=[
            pltpu.VMEM((2048, A), BF),
            pltpu.VMEM((2048, B), BF),
            pltpu.VMEM((128, 4, 256), BF),
            cache_like,
            cache_like,
            cache_like,
            pltpu.VMEM((128, 2048), BF),
            pltpu.VMEM((128, A), F32),
            pltpu.VMEM((640, 128), BF),
            pltpu.VMEM((NY, 32, 256), BF),
            pltpu.VMEM((NY, 32, 256), BF),
            pltpu.VMEM((NY, 32, 2048), BF),
            pltpu.VMEM((NY, 32, 2048), BF),
            dma, many, dma, many, dma, dma, dma, dma, dma, dma, dma, dma, dma, dma,
        ],
        compiler_params=pltpu.CompilerParams(collective_id=0, has_side_effects=True),
        name="block",
    )(*args)


def shards(tokens, attn_gain, q_gain, k_gain, ffn_gain, w_query, w_keyval, w_out, prior_cache, prior_len, stretch_len):
    seq_index = lax.axis_index("seq")
    length = tokens.shape[1]
    prior_count = lax.dynamic_index_in_dim(prior_len, seq_index, keepdims=False)
    positions = (prior_count + jnp.arange(length, dtype=jnp.int32)).astype(F32)
    middle = HD // 2
    inverse = jnp.exp(jnp.arange(middle, dtype=F32) * (-2.0 * math.log(10000.0) / HD))
    angles = positions[:, None] * inverse[None, :]
    cosine, sine = jnp.cos(angles), jnp.sin(angles)
    cosine = jnp.concatenate([cosine] * 4, axis=1)
    sine = jnp.concatenate([-sine, sine, -sine, sine], axis=1)

    def twice(gain):
        return jnp.concatenate([gain, gain])[None].astype(F32)

    hidden, ffn, fresh, decode = block(
        tokens[0],
        attn_gain[None].astype(F32),
        twice(q_gain),
        twice(k_gain),
        ffn_gain[None].astype(F32),
        w_query,
        w_keyval,
        w_out.T,
        prior_cache,
        cosine,
        sine,
        prior_len,
        stretch_len,
    )
    return (hidden[None], ffn[None], fresh[None], decode[None])


def solution(mesh):
    placed = (
        P("seq", None, None),
        P(),
        P(),
        P(),
        P(),
        P("seq", "head"),
        P("seq", None),
        P("head", "seq"),
        P(None, "seq", None),
        P(),
        P(),
    )
    return jax.shard_map(
        shards,
        mesh=mesh,
        in_specs=placed,
        out_specs=(P("seq", "head", None),) * 4,
        check_vma=False,
    )
```

```python
import math

import jax
import jax.numpy as jnp
from jax import lax
from jax.experimental import pallas as pl
from jax.experimental.pallas import tpu as pltpu
from jax.sharding import PartitionSpec as P

HD = 64
NX, NZ, NY = 4, 16, 4
PLANE = NZ * 2
A, B = 640, 256
MESH = pl.DeviceIdType.MESH
BF = jnp.bfloat16
F32 = jnp.float32
epsilon = 1e-06


def body(
    tok, again, qgain, kgain, fgain, wq, wkv, wo, cache, prior, stretch,
    hidden, ffn, fresh, decode,
    wa, wb, cpack, xb, eb, yb, normed, acc, qs, kvs, kvr, tb, rb, cosine, sine,
    a_send, a_recv, b_send, b_recv, x_send, x_recv, e_send, e_recv, y_send, y_recv, k_send, k_recv, t_send, t_recv,
):
    s = lax.axis_index("seq")
    h = lax.axis_index("head")
    x = s // PLANE
    low = lax.rem(s, PLANE)
    z = low // 2
    c = lax.rem(low, 2)

    def sid(xx, zz, cc):
        return xx * PLANE + zz * 2 + cc

    def wrapx(v):
        return lax.rem(v + NX, NX)

    def wrapz(v):
        return lax.rem(v + NZ, NZ)

    barrier = pltpu.get_barrier_semaphore()

    def signal(target):
        pl.semaphore_signal(barrier, inc=1, device_id=target, device_id_type=MESH)

    def greet(k, carry):
        signal({"seq": x * PLANE + lax.rem(low + k, PLANE)})
        return carry

    lax.fori_loop(1, PLANE, greet, 0)
    for k in range(1, NX):
        signal({"seq": sid(wrapx(x + k), z, c)})
    for k in range(1, NY):
        signal({"head": lax.rem(h + k, NY)})

    own = pl.ds(pl.multiple_of(s * 16, 16), 16)
    for head in range(NY):

        @pl.when(h == head)
        def _(head=head):
            lo = 64 * head
            wa[own, 0:128] = wkv[:, lo : lo + 128]
            wa[own, 128:256] = wkv[:, 320 + lo : 448 + lo]

    wa[own, 256:640] = jnp.concatenate([wq[...], wo[:, 0:64]], axis=1)
    wb[own, :] = wo[:, 64:320]

    pl.semaphore_wait(barrier, PLANE - 1 + NX - 1 + NY - 1)

    ahead = jnp.where(c == 0, 1, -1)
    partner = {"seq": sid(x, z, 1 - c)}

    def tox(d):
        return {"seq": sid(wrapx(x + d), z, c)}

    def toz(d):
        return {"seq": sid(x, wrapz(z + d), c)}

    class Ring:
        def __init__(self, buf, send, recv):
            self.buf, self.send, self.recv, self.count = buf, send, recv, 0

        def rows(self, b):
            return self.buf.at[pl.ds(pl.multiple_of(b * 16, 16), 16)]

        def push(self, b, target):
            self.count += 1
            pltpu.make_async_remote_copy(
                src_ref=self.rows(b),
                dst_ref=self.rows(b),
                send_sem=self.send,
                recv_sem=self.recv.at[b],
                device_id=target,
                device_id_type=MESH,
            ).start()

        def arrive(self, b):
            pltpu.make_async_copy(self.rows(b), self.rows(b), self.recv.at[b]).wait()

        def spread(self, b):
            self.push(b, tox(ahead))
            self.push(b, tox(-ahead))
            self.push(b, partner)

        def near(self, b):
            for d in (2, -2, 1, -1):
                self.push(b, toz(d))

        def start(self):
            for d in (5, -5, 8):
                self.push(s, toz(d))
            self.near(s)
            self.spread(s)

        def here(self, d, far=False):
            b = sid(x, wrapz(z + d), c)
            self.arrive(b)
            if far:
                self.near(b)
            self.spread(b)

        def relay(self, d):
            b = sid(wrapx(x - ahead), wrapz(z + d), c)
            self.arrive(b)
            self.push(b, tox(ahead))
            self.push(b, partner)
            b = sid(wrapx(x + ahead), wrapz(z + d), c)
            self.arrive(b)
            self.push(b, partner)

        def last(self, d):
            b = sid(wrapx(x + 2), wrapz(z + d), c)
            self.arrive(b)
            self.push(b, partner)

        def shared(self, xx):
            def one(zz, carry):
                self.arrive(sid(xx, zz, 1 - c))
                return carry

            lax.fori_loop(0, NZ, one, 0)

        def drain(self):
            left = self.count
            while left > 0:
                n = min(left, 128)
                part = self.buf.at[pl.ds(0, n * 16)]
                pltpu.make_async_copy(part, part, self.send).wait()
                left -= n

    ra, rbq = Ring(wa, a_send, a_recv), Ring(wb, b_send, b_recv)
    ra.start()
    for head in range(NY):

        @pl.when(h == head)
        def _(head=head):
            lo = 64 * head

            def pack(i, carry):
                at = pl.ds(pl.multiple_of(i * 16, 16), 16)
                cpack[at, :, 0:128] = cache[at, :, lo : lo + 128]
                cpack[at, :, 128:256] = cache[at, :, 320 + lo : 448 + lo]
                return carry

            lax.fori_loop(0, 8, pack, 0)

    prior_count = prior[s]
    pair_lane = lax.rem(lax.broadcasted_iota(jnp.int32, (128, 128), 1), 64)
    inverse = jnp.exp(lax.rem(pair_lane, 32).astype(F32) * (-2.0 * math.log(10000.0) / HD))
    angles = (prior_count + lax.broadcasted_iota(jnp.int32, (128, 128), 0)).astype(F32) * inverse
    cosine[...] = jnp.cos(angles)
    sines = jnp.sin(angles)
    sine[...] = jnp.where(pair_lane < 32, -sines, sines)
    for k in (2, 1, 3):
        xx = wrapx(x + k)
        pltpu.make_async_remote_copy(
            src_ref=cpack.at[pl.ds(pl.multiple_of(xx * PLANE, PLANE), PLANE)],
            dst_ref=xb.at[x],
            send_sem=x_send,
            recv_sem=x_recv,
            device_id=tox(k),
            device_id_type=MESH,
        ).start()
    pltpu.make_async_copy(cpack.at[pl.ds(pl.multiple_of(x * PLANE, PLANE), PLANE)], xb.at[x], x_recv).start()
    def norm(i, carry):
        at = pl.ds(pl.multiple_of(i * 16, 16), 16)
        v = tok[at, :].astype(F32)
        v = v * lax.rsqrt(jnp.mean(v * v, axis=-1, keepdims=True) + epsilon) * again[...].astype(F32)[None, :]
        normed[at, :] = v.astype(BF)
        return carry

    lax.fori_loop(0, 8, norm, 0)
    near, far = (1, -1, 2, -2), (5, -5)
    rest = (4, -4, 6, -6, 3, -3, 7, -7)
    for d in near:
        ra.here(d)
    ra.relay(0)
    for d in far:
        ra.here(d, True)
    pltpu.make_async_copy(xb, xb, x_recv).wait()

    def hand(k, carry):
        to = lax.rem(low + k, PLANE)
        pltpu.make_async_remote_copy(
            src_ref=xb.at[:, to],
            dst_ref=eb.at[:, low],
            send_sem=e_send,
            recv_sem=e_recv,
            device_id={"seq": x * PLANE + to},
            device_id_type=MESH,
        ).start()
        return carry

    lax.fori_loop(1, PLANE, hand, 0)
    pltpu.make_async_copy(xb.at[:, low], eb.at[:, low], e_recv).start()
    rbq.start()
    for d in near:
        ra.relay(d)
    ra.last(0)
    ra.here(8)
    for d in rest:
        ra.here(d)
    for d in far:
        ra.relay(d)
    for d in near:
        ra.last(d)
    for d in near:
        rbq.here(d)
    for d in far:
        rbq.here(d, True)
    ra.relay(8)
    for d in rest:
        ra.relay(d)
    for d in far:
        ra.last(d)
    rbq.relay(0)
    ra.shared(x)

    def project(xx, first=False):
        deep = pl.ds(pl.multiple_of(xx * 512, 512), 512)
        part = jnp.dot(normed[:, deep], wa[deep, :], preferred_element_type=F32)
        if first:
            acc[...] = part
        else:
            acc[...] += part

    project(x, True)
    ra.last(8)
    for d in rest:
        ra.last(d)
    rbq.here(8)
    for d in rest:
        rbq.here(d)
    ra.shared(wrapx(x + 1))
    project(wrapx(x + 1))
    ra.shared(wrapx(x - 1))
    project(wrapx(x - 1))
    for d in near:
        rbq.relay(d)
    rbq.last(0)
    for d in far:
        rbq.relay(d)
    for d in near:
        rbq.last(d)
    ra.shared(wrapx(x + 2))
    project(wrapx(x + 2))
    rbq.relay(8)
    for d in rest:
        rbq.relay(d)

    lane = lax.broadcasted_iota(jnp.int32, (128, 128), 1)
    row = lax.broadcasted_iota(jnp.int32, (128, 128), 0)
    upper = lane >= 64
    flip = lax.rem(lane, 64) < 32

    def position(t, gain):
        sq = t * t
        lo = jnp.sum(jnp.where(upper, 0.0, sq), axis=-1, keepdims=True)
        hi = jnp.sum(jnp.where(upper, sq, 0.0), axis=-1, keepdims=True)
        v = t * lax.rsqrt(jnp.where(upper, hi, lo) * (1.0 / 64) + epsilon) * gain
        turned = jnp.where(flip, pltpu.roll(v, 96, 1), pltpu.roll(v, 32, 1))
        return v * cosine[...] + turned * sine[...]

    def twice(gain):
        g = gain[...].astype(F32)[None, :]
        return jnp.concatenate([g, g], axis=1)

    keys = position(acc[:, 0:128], twice(kgain)).astype(BF)
    values = acc[:, 128:256].astype(BF)
    kvs[:, :, 0:128] = keys.reshape(NY, 32, 128)
    kvs[:, :, 128:256] = values.reshape(NY, 32, 128)
    kvr[h] = kvs[h]
    for k in (2, 1, 3):
        to = lax.rem(h + k, NY)
        pltpu.make_async_remote_copy(
            src_ref=kvs.at[to],
            dst_ref=kvr.at[h],
            send_sem=k_send,
            recv_sem=k_recv,
            device_id={"head": to},
            device_id_type=MESH,
        ).start()
    second = [jnp.where(i >= 4 - h, 1, 0) for i in range(5)]
    for pair in range(3):
        t = position(acc[:, 256 + 128 * pair : 384 + 128 * pair], twice(qgain))
        r = pltpu.roll(t, 64, 1)
        for half in range(2):
            i = 2 * pair + half
            if i < 5:
                v = jnp.where(second[i] == half, t, r)
                v = jnp.where(jnp.where(upper, 1, 0) == second[i], v, 0.0)
                qs[128 * i : 128 * (i + 1), :] = v.astype(BF)

    pltpu.make_async_copy(eb, eb, e_recv).wait()
    for k in (2, 1, 3):
        to = lax.rem(h + k, NY)
        pltpu.make_async_remote_copy(
            src_ref=eb.at[to],
            dst_ref=yb.at[h],
            send_sem=y_send,
            recv_sem=y_recv,
            device_id={"head": to},
            device_id_type=MESH,
        ).start()
    pltpu.make_async_copy(eb.at[h], yb.at[h], y_recv).start()
    stored = [eb[p].reshape(128, 256) for p in range(4)]
    all_keys = jnp.concatenate([t[:, 0:128] for t in stored] + [keys], axis=0)
    all_values = jnp.concatenate([t[:, 128:256] for t in stored] + [values], axis=0)
    slot = lax.broadcasted_iota(jnp.int32, (128, 512), 1)
    earlier = slot < prior_count
    causal = lane <= row
    allowed = jnp.concatenate([earlier, causal], axis=1)
    heads = []
    for i in range(5):
        sc = lax.dot_general(
            qs[128 * i : 128 * (i + 1), :], all_keys, (((1,), (1,)), ((), ())), preferred_element_type=F32
        ) * (1.0 / math.sqrt(HD))
        sc = jnp.where(allowed, sc, -jnp.inf)
        w = jnp.exp(sc - jnp.max(sc, axis=-1, keepdims=True))
        total = jnp.sum(w, axis=-1, keepdims=True)
        m = jnp.dot(w.astype(BF), all_values, preferred_element_type=F32) / total
        heads.append(jnp.where(second[i] == (i + 1) % 2, m, pltpu.roll(m, 64, 1)))
    att = [
        jnp.where(upper, heads[0], 0.0).astype(BF),
        jnp.where(upper, heads[2], heads[1]).astype(BF),
        jnp.where(upper, heads[4], heads[3]).astype(BF),
    ]
    att12 = jnp.concatenate(att[1:], axis=1)

    def project_out(xx):
        wide = pl.ds(pl.multiple_of(xx * 512, 512), 512)
        dims = (((1,), (1,)), ((), ()))
        part = lax.dot_general(att[0], wa[wide, 512:640], dims, preferred_element_type=F32)
        part = part + lax.dot_general(att12, wb[wide, :], dims, preferred_element_type=F32)
        tb[:, :, wide] = part.astype(BF).reshape(NY, 32, 512)
        for k in (2, 1, 3):
            to = lax.rem(h + k, NY)
            pltpu.make_async_remote_copy(
                src_ref=tb.at[to, :, wide],
                dst_ref=rb.at[h, :, wide],
                send_sem=t_send,
                recv_sem=t_recv,
                device_id={"head": to},
                device_id_type=MESH,
            ).start()

    rbq.shared(x)
    project_out(x)
    for d in far + (8,) + rest:
        rbq.last(d)
    for d in (1, -1, 2):
        rbq.shared(wrapx(x + d))
        project_out(wrapx(x + d))

    limit = stretch[s]

    def assemble(t0, t1, t2, t3):
        low_half = lax.broadcasted_iota(jnp.int32, (t0.shape[0], 128), 1) < 64
        mid = pltpu.roll(jnp.where(low_half, t0[:, 128:256].astype(F32), t3[:, 0:128].astype(F32)), 64, 1).astype(BF)
        return jnp.concatenate([t0[:, 0:128], t2[:, 0:128], mid, t1[:, 128:256], t3[:, 128:256]], axis=1)

    pltpu.make_async_copy(yb, yb, y_recv).wait()
    decode[...] = assemble(*[yb[p].reshape(128, 256) for p in range(4)])
    three = kvr.at[pl.ds(0, 3)]
    pltpu.make_async_copy(three, three, k_recv).wait()
    rows = h * 32 + lax.broadcasted_iota(jnp.int32, (32, 640), 0)
    made = assemble(*[kvr[p] for p in range(4)])
    fresh[...] = jnp.where(rows < limit, made, jnp.zeros_like(made))

    three = rb.at[pl.ds(0, 3)]
    pltpu.make_async_copy(three, three, t_recv).wait()
    summed = tok[pl.ds(pl.multiple_of(h * 32, 32), 32), :].astype(F32)
    share = tb[h].astype(F32)
    for k in range(1, NY):
        share = share + rb[lax.rem(h + k, NY)].astype(F32)
    resid = summed + share
    valid = h * 32 + lax.broadcasted_iota(jnp.int32, (32, 2048), 0) < limit
    hidden[...] = jnp.where(valid, resid, 0.0).astype(BF)
    scaled = resid * lax.rsqrt(jnp.mean(resid * resid, axis=-1, keepdims=True) + epsilon) * fgain[...].astype(F32)[None, :]
    ffn[...] = jnp.where(valid, scaled, 0.0).astype(BF)

    for ref, sem in ((xb.at[pl.ds(0, 3)], x_send), (eb.at[:, pl.ds(0, PLANE - 1)], e_send),
                     (yb.at[pl.ds(0, 3)], y_send), (kvr.at[pl.ds(0, 3)], k_send), (rb.at[pl.ds(0, 3)], t_send)):
        pltpu.make_async_copy(ref, ref, sem).wait()
    ra.drain()
    rbq.drain()


def block(*args):
    vmem = pl.BlockSpec(memory_space=pltpu.VMEM)
    smem = pl.BlockSpec(memory_space=pltpu.SMEM)
    dma = pltpu.SemaphoreType.DMA
    many = pltpu.SemaphoreType.DMA((NX * PLANE,))
    cache_like = pltpu.VMEM((NX, PLANE, 4, 256), BF)
    return pl.pallas_call(
        body,
        out_shape=(
            jax.ShapeDtypeStruct((32, 2048), BF),
            jax.ShapeDtypeStruct((32, 2048), BF),
            jax.ShapeDtypeStruct((32, 640), BF),
            jax.ShapeDtypeStruct((128, 640), BF),
        ),
        in_specs=[vmem] * 9 + [smem] * 2,
        out_specs=(vmem,) * 4,
        scratch_shapes=[
            pltpu.VMEM((2048, A), BF),
            pltpu.VMEM((2048, B), BF),
            pltpu.VMEM((128, 4, 256), BF),
            cache_like,
            cache_like,
            cache_like,
            pltpu.VMEM((128, 2048), BF),
            pltpu.VMEM((128, A), F32),
            pltpu.VMEM((640, 128), BF),
            pltpu.VMEM((NY, 32, 256), BF),
            pltpu.VMEM((NY, 32, 256), BF),
            pltpu.VMEM((NY, 32, 2048), BF),
            pltpu.VMEM((NY, 32, 2048), BF),
            pltpu.VMEM((128, 128), F32),
            pltpu.VMEM((128, 128), F32),
            dma, many, dma, many, dma, dma, dma, dma, dma, dma, dma, dma, dma, dma,
        ],
        compiler_params=pltpu.CompilerParams(collective_id=0, has_side_effects=True),
        name="block",
    )(*args)


def settle_body(*refs):
    for src, dst in zip(refs[:4], refs[4:]):
        dst[...] = src[...]


def settle(*made):
    vmem = pl.BlockSpec(memory_space=pltpu.VMEM)
    return pl.pallas_call(
        settle_body,
        out_shape=[jax.ShapeDtypeStruct(v.shape, v.dtype) for v in made],
        in_specs=[vmem] * 4,
        out_specs=[vmem] * 4,
        name="settle",
    )(*made)


def shards(tokens, attn_gain, q_gain, k_gain, ffn_gain, w_query, w_keyval, w_out, prior_cache, prior_len, stretch_len):
    made = block(
        tokens[0], attn_gain, q_gain, k_gain, ffn_gain, w_query, w_keyval, w_out.T, prior_cache, prior_len, stretch_len
    )
    return tuple(v[None] for v in settle(*made))


def solution(mesh):
    placed = (
        P("seq", None, None),
        P(),
        P(),
        P(),
        P(),
        P("seq", "head"),
        P("seq", None),
        P("head", "seq"),
        P(None, "seq", None),
        P(),
        P(),
    )
    return jax.shard_map(
        shards,
        mesh=mesh,
        in_specs=placed,
        out_specs=(P("seq", "head", None),) * 4,
        check_vma=False,
    )
```

```python
import math

import jax
import jax.numpy as jnp
from jax import lax
from jax.experimental import pallas as pl
from jax.experimental.pallas import tpu as pltpu
from jax.sharding import PartitionSpec as P

HD = 64
NX, NZ, NY = 4, 16, 4
PLANE = NZ * 2
A, B = 640, 256
MESH = pl.DeviceIdType.MESH
BF = jnp.bfloat16
F32 = jnp.float32
epsilon = 1e-06


def body(
    tok, again, qgain, kgain, fgain, wq, wkv, wo, cache, prior, stretch,
    hidden, ffn, fresh, decode,
    wa, wb, cpack, xb, eb, yb, normed, acc, qs, kvs, kvr, tb, rb, cosine, sine,
    a_send, a_recv, b_send, b_recv, x_send, x_recv, e_send, e_recv, y_send, y_recv, k_send, k_recv, t_send, t_recv,
):
    s = lax.axis_index("seq")
    h = lax.axis_index("head")
    x = s // PLANE
    low = lax.rem(s, PLANE)
    z = low // 2
    c = lax.rem(low, 2)

    def sid(xx, zz, cc):
        return xx * PLANE + zz * 2 + cc

    def wrapx(v):
        return lax.rem(v + NX, NX)

    def wrapz(v):
        return lax.rem(v + NZ, NZ)

    barrier = pltpu.get_barrier_semaphore()

    def signal(target):
        pl.semaphore_signal(barrier, inc=1, device_id=target, device_id_type=MESH)

    def greet(k, carry):
        signal({"seq": x * PLANE + lax.rem(low + k, PLANE)})
        return carry

    lax.fori_loop(1, PLANE, greet, 0)
    for k in range(1, NX):
        signal({"seq": sid(wrapx(x + k), z, c)})
    for k in range(1, NY):
        signal({"head": lax.rem(h + k, NY)})

    own = pl.ds(pl.multiple_of(s * 16, 16), 16)
    for head in range(NY):

        @pl.when(h == head)
        def _(head=head):
            lo = 64 * head
            wa[own, 0:128] = wkv[:, lo : lo + 128]
            wa[own, 128:256] = wkv[:, 320 + lo : 448 + lo]

    wa[own, 256:640] = jnp.concatenate([wq[...], wo[:, 0:64]], axis=1)
    wb[own, :] = wo[:, 64:320]

    pl.semaphore_wait(barrier, PLANE - 1 + NX - 1 + NY - 1)

    ahead = jnp.where(c == 0, 1, -1)
    partner = {"seq": sid(x, z, 1 - c)}

    def tox(d):
        return {"seq": sid(wrapx(x + d), z, c)}

    def toz(d):
        return {"seq": sid(x, wrapz(z + d), c)}

    class Ring:
        def __init__(self, buf, send, recv):
            self.buf, self.send, self.recv, self.count = buf, send, recv, 0

        def rows(self, b):
            return self.buf.at[pl.ds(pl.multiple_of(b * 16, 16), 16)]

        def push(self, b, target):
            self.count += 1
            pltpu.make_async_remote_copy(
                src_ref=self.rows(b),
                dst_ref=self.rows(b),
                send_sem=self.send,
                recv_sem=self.recv.at[b],
                device_id=target,
                device_id_type=MESH,
            ).start()

        def arrive(self, b):
            pltpu.make_async_copy(self.rows(b), self.rows(b), self.recv.at[b]).wait()

        def spread(self, b):
            self.push(b, tox(ahead))
            self.push(b, tox(-ahead))
            self.push(b, partner)

        def near(self, b):
            for d in (2, -2, 1, -1):
                self.push(b, toz(d))

        def start(self):
            for d in (5, -5, 8):
                self.push(s, toz(d))
            self.near(s)
            self.spread(s)

        def here(self, d, far=False):
            b = sid(x, wrapz(z + d), c)
            self.arrive(b)
            if far:
                self.near(b)
            self.spread(b)

        def hop(self, d):
            b = sid(x, wrapz(z + d), c)
            self.arrive(b)
            self.near(b)

        def out(self, d):
            self.spread(sid(x, wrapz(z + d), c))

        def relay(self, d):
            b = sid(wrapx(x - ahead), wrapz(z + d), c)
            self.arrive(b)
            self.push(b, tox(ahead))
            self.push(b, partner)
            b = sid(wrapx(x + ahead), wrapz(z + d), c)
            self.arrive(b)
            self.push(b, partner)

        def last(self, d):
            b = sid(wrapx(x + 2), wrapz(z + d), c)
            self.arrive(b)
            self.push(b, partner)

        def shared(self, xx):
            def one(zz, carry):
                self.arrive(sid(xx, zz, 1 - c))
                return carry

            lax.fori_loop(0, NZ, one, 0)

        def drain(self):
            left = self.count
            while left > 0:
                n = min(left, 128)
                part = self.buf.at[pl.ds(0, n * 16)]
                pltpu.make_async_copy(part, part, self.send).wait()
                left -= n

    ra, rbq = Ring(wa, a_send, a_recv), Ring(wb, b_send, b_recv)
    ra.start()
    for head in range(NY):

        @pl.when(h == head)
        def _(head=head):
            lo = 64 * head

            def pack(i, carry):
                at = pl.ds(pl.multiple_of(i * 16, 16), 16)
                cpack[at, :, 0:128] = cache[at, :, lo : lo + 128]
                cpack[at, :, 128:256] = cache[at, :, 320 + lo : 448 + lo]
                return carry

            lax.fori_loop(0, 8, pack, 0)

    prior_count = prior[s]
    pair_lane = lax.rem(lax.broadcasted_iota(jnp.int32, (128, 128), 1), 64)
    inverse = jnp.exp(lax.rem(pair_lane, 32).astype(F32) * (-2.0 * math.log(10000.0) / HD))
    angles = (prior_count + lax.broadcasted_iota(jnp.int32, (128, 128), 0)).astype(F32) * inverse
    cosine[...] = jnp.cos(angles)
    sines = jnp.sin(angles)
    sine[...] = jnp.where(pair_lane < 32, -sines, sines)
    for k in (2, 1, 3):
        xx = wrapx(x + k)
        pltpu.make_async_remote_copy(
            src_ref=cpack.at[pl.ds(pl.multiple_of(xx * PLANE, PLANE), PLANE)],
            dst_ref=xb.at[x],
            send_sem=x_send,
            recv_sem=x_recv,
            device_id=tox(k),
            device_id_type=MESH,
        ).start()
    pltpu.make_async_copy(cpack.at[pl.ds(pl.multiple_of(x * PLANE, PLANE), PLANE)], xb.at[x], x_recv).start()
    near, far = (1, -1, 2, -2), (5, -5)
    rest = (4, -4, 6, -6, 3, -3, 7, -7)
    rbq.start()
    def norm(i, carry):
        at = pl.ds(pl.multiple_of(i * 16, 16), 16)
        v = tok[at, :].astype(F32)
        v = v * lax.rsqrt(jnp.mean(v * v, axis=-1, keepdims=True) + epsilon) * again[...].astype(F32)[None, :]
        normed[at, :] = v.astype(BF)
        return carry

    lax.fori_loop(0, 8, norm, 0)
    for d in near:
        ra.here(d)
    ra.relay(0)
    for d in far:
        ra.here(d, True)
    for d in far:
        rbq.hop(d)
    pltpu.make_async_copy(xb, xb, x_recv).wait()

    def hand(k, carry):
        to = lax.rem(low + k, PLANE)
        pltpu.make_async_remote_copy(
            src_ref=xb.at[:, to],
            dst_ref=eb.at[:, low],
            send_sem=e_send,
            recv_sem=e_recv,
            device_id={"seq": x * PLANE + to},
            device_id_type=MESH,
        ).start()
        return carry

    lax.fori_loop(1, PLANE, hand, 0)
    pltpu.make_async_copy(xb.at[:, low], eb.at[:, low], e_recv).start()
    for d in near:
        ra.relay(d)
    ra.last(0)
    ra.here(8)
    for d in rest:
        ra.here(d)
    for d in far:
        ra.relay(d)
    for d in near:
        ra.last(d)
    for d in near:
        rbq.here(d)
    for d in far:
        rbq.out(d)
    ra.relay(8)
    for d in rest:
        ra.relay(d)
    for d in far:
        ra.last(d)
    rbq.relay(0)
    ra.shared(x)

    def project(xx, first=False):
        deep = pl.ds(pl.multiple_of(xx * 512, 512), 512)
        part = jnp.dot(normed[:, deep], wa[deep, :], preferred_element_type=F32)
        if first:
            acc[...] = part
        else:
            acc[...] += part

    project(x, True)
    ra.last(8)
    for d in rest:
        ra.last(d)
    rbq.here(8)
    for d in rest:
        rbq.here(d)
    ra.shared(wrapx(x + 1))
    project(wrapx(x + 1))
    ra.shared(wrapx(x - 1))
    project(wrapx(x - 1))
    for d in near:
        rbq.relay(d)
    rbq.last(0)
    for d in far:
        rbq.relay(d)
    for d in near:
        rbq.last(d)
    ra.shared(wrapx(x + 2))
    project(wrapx(x + 2))
    rbq.relay(8)
    for d in rest:
        rbq.relay(d)

    lane = lax.broadcasted_iota(jnp.int32, (128, 128), 1)
    row = lax.broadcasted_iota(jnp.int32, (128, 128), 0)
    upper = lane >= 64
    flip = lax.rem(lane, 64) < 32

    def position(t, gain):
        sq = t * t
        lo = jnp.sum(jnp.where(upper, 0.0, sq), axis=-1, keepdims=True)
        hi = jnp.sum(jnp.where(upper, sq, 0.0), axis=-1, keepdims=True)
        v = t * lax.rsqrt(jnp.where(upper, hi, lo) * (1.0 / 64) + epsilon) * gain
        turned = jnp.where(flip, pltpu.roll(v, 96, 1), pltpu.roll(v, 32, 1))
        return v * cosine[...] + turned * sine[...]

    def twice(gain):
        g = gain[...].astype(F32)[None, :]
        return jnp.concatenate([g, g], axis=1)

    keys = position(acc[:, 0:128], twice(kgain)).astype(BF)
    values = acc[:, 128:256].astype(BF)
    kvs[:, :, 0:128] = keys.reshape(NY, 32, 128)
    kvs[:, :, 128:256] = values.reshape(NY, 32, 128)
    kvr[h] = kvs[h]
    for k in (2, 1, 3):
        to = lax.rem(h + k, NY)
        pltpu.make_async_remote_copy(
            src_ref=kvs.at[to],
            dst_ref=kvr.at[h],
            send_sem=k_send,
            recv_sem=k_recv,
            device_id={"head": to},
            device_id_type=MESH,
        ).start()
    second = [jnp.where(i >= 4 - h, 1, 0) for i in range(5)]
    for pair in range(3):
        t = position(acc[:, 256 + 128 * pair : 384 + 128 * pair], twice(qgain))
        r = pltpu.roll(t, 64, 1)
        for half in range(2):
            i = 2 * pair + half
            if i < 5:
                v = jnp.where(second[i] == half, t, r)
                v = jnp.where(jnp.where(upper, 1, 0) == second[i], v, 0.0)
                qs[128 * i : 128 * (i + 1), :] = v.astype(BF)

    pltpu.make_async_copy(eb, eb, e_recv).wait()
    for k in (2, 1, 3):
        to = lax.rem(h + k, NY)
        pltpu.make_async_remote_copy(
            src_ref=eb.at[to],
            dst_ref=yb.at[h],
            send_sem=y_send,
            recv_sem=y_recv,
            device_id={"head": to},
            device_id_type=MESH,
        ).start()
    pltpu.make_async_copy(eb.at[h], yb.at[h], y_recv).start()
    stored = [eb[p].reshape(128, 256) for p in range(4)]
    all_keys = jnp.concatenate([t[:, 0:128] for t in stored] + [keys], axis=0)
    all_values = jnp.concatenate([t[:, 128:256] for t in stored] + [values], axis=0)
    slot = lax.broadcasted_iota(jnp.int32, (128, 512), 1)
    earlier = slot < prior_count
    causal = lane <= row
    allowed = jnp.concatenate([earlier, causal], axis=1)
    heads = []
    for i in range(5):
        sc = lax.dot_general(
            qs[128 * i : 128 * (i + 1), :], all_keys, (((1,), (1,)), ((), ())), preferred_element_type=F32
        ) * (1.0 / math.sqrt(HD))
        sc = jnp.where(allowed, sc, -jnp.inf)
        w = jnp.exp(sc - jnp.max(sc, axis=-1, keepdims=True))
        total = jnp.sum(w, axis=-1, keepdims=True)
        m = jnp.dot(w.astype(BF), all_values, preferred_element_type=F32) / total
        heads.append(jnp.where(second[i] == (i + 1) % 2, m, pltpu.roll(m, 64, 1)))
    att = [
        jnp.where(upper, heads[0], 0.0).astype(BF),
        jnp.where(upper, heads[2], heads[1]).astype(BF),
        jnp.where(upper, heads[4], heads[3]).astype(BF),
    ]
    att12 = jnp.concatenate(att[1:], axis=1)

    def project_out(xx):
        wide = pl.ds(pl.multiple_of(xx * 512, 512), 512)
        dims = (((1,), (1,)), ((), ()))
        part = lax.dot_general(att[0], wa[wide, 512:640], dims, preferred_element_type=F32)
        part = part + lax.dot_general(att12, wb[wide, :], dims, preferred_element_type=F32)
        tb[:, :, wide] = part.astype(BF).reshape(NY, 32, 512)
        for k in (2, 1, 3):
            to = lax.rem(h + k, NY)
            pltpu.make_async_remote_copy(
                src_ref=tb.at[to, :, wide],
                dst_ref=rb.at[h, :, wide],
                send_sem=t_send,
                recv_sem=t_recv,
                device_id={"head": to},
                device_id_type=MESH,
            ).start()

    rbq.shared(x)
    project_out(x)
    for d in far + (8,) + rest:
        rbq.last(d)
    for d in (1, -1, 2):
        rbq.shared(wrapx(x + d))
        project_out(wrapx(x + d))

    limit = stretch[s]

    def assemble(t0, t1, t2, t3):
        low_half = lax.broadcasted_iota(jnp.int32, (t0.shape[0], 128), 1) < 64
        mid = pltpu.roll(jnp.where(low_half, t0[:, 128:256].astype(F32), t3[:, 0:128].astype(F32)), 64, 1).astype(BF)
        return jnp.concatenate([t0[:, 0:128], t2[:, 0:128], mid, t1[:, 128:256], t3[:, 128:256]], axis=1)

    pltpu.make_async_copy(yb, yb, y_recv).wait()
    decode[...] = assemble(*[yb[p].reshape(128, 256) for p in range(4)])
    three = kvr.at[pl.ds(0, 3)]
    pltpu.make_async_copy(three, three, k_recv).wait()
    rows = h * 32 + lax.broadcasted_iota(jnp.int32, (32, 640), 0)
    made = assemble(*[kvr[p] for p in range(4)])
    fresh[...] = jnp.where(rows < limit, made, jnp.zeros_like(made))

    three = rb.at[pl.ds(0, 3)]
    pltpu.make_async_copy(three, three, t_recv).wait()
    summed = tok[pl.ds(pl.multiple_of(h * 32, 32), 32), :].astype(F32)
    share = tb[h].astype(F32)
    for k in range(1, NY):
        share = share + rb[lax.rem(h + k, NY)].astype(F32)
    resid = summed + share
    valid = h * 32 + lax.broadcasted_iota(jnp.int32, (32, 2048), 0) < limit
    hidden[...] = jnp.where(valid, resid, 0.0).astype(BF)
    scaled = resid * lax.rsqrt(jnp.mean(resid * resid, axis=-1, keepdims=True) + epsilon) * fgain[...].astype(F32)[None, :]
    ffn[...] = jnp.where(valid, scaled, 0.0).astype(BF)

    for ref, sem in ((xb.at[pl.ds(0, 3)], x_send), (eb.at[:, pl.ds(0, PLANE - 1)], e_send),
                     (yb.at[pl.ds(0, 3)], y_send), (kvr.at[pl.ds(0, 3)], k_send), (rb.at[pl.ds(0, 3)], t_send)):
        pltpu.make_async_copy(ref, ref, sem).wait()
    ra.drain()
    rbq.drain()


def block(*args):
    vmem = pl.BlockSpec(memory_space=pltpu.VMEM)
    smem = pl.BlockSpec(memory_space=pltpu.SMEM)
    dma = pltpu.SemaphoreType.DMA
    many = pltpu.SemaphoreType.DMA((NX * PLANE,))
    cache_like = pltpu.VMEM((NX, PLANE, 4, 256), BF)
    return pl.pallas_call(
        body,
        out_shape=(
            jax.ShapeDtypeStruct((32, 2048), BF),
            jax.ShapeDtypeStruct((32, 2048), BF),
            jax.ShapeDtypeStruct((32, 640), BF),
            jax.ShapeDtypeStruct((128, 640), BF),
        ),
        in_specs=[vmem] * 9 + [smem] * 2,
        out_specs=(vmem,) * 4,
        scratch_shapes=[
            pltpu.VMEM((2048, A), BF),
            pltpu.VMEM((2048, B), BF),
            pltpu.VMEM((128, 4, 256), BF),
            cache_like,
            cache_like,
            cache_like,
            pltpu.VMEM((128, 2048), BF),
            pltpu.VMEM((128, A), F32),
            pltpu.VMEM((640, 128), BF),
            pltpu.VMEM((NY, 32, 256), BF),
            pltpu.VMEM((NY, 32, 256), BF),
            pltpu.VMEM((NY, 32, 2048), BF),
            pltpu.VMEM((NY, 32, 2048), BF),
            pltpu.VMEM((128, 128), F32),
            pltpu.VMEM((128, 128), F32),
            dma, many, dma, many, dma, dma, dma, dma, dma, dma, dma, dma, dma, dma,
        ],
        compiler_params=pltpu.CompilerParams(collective_id=0, has_side_effects=True),
        name="block",
    )(*args)


def settle_body(*refs):
    for src, dst in zip(refs[:4], refs[4:]):
        dst[...] = src[...]


def settle(*made):
    vmem = pl.BlockSpec(memory_space=pltpu.VMEM)
    return pl.pallas_call(
        settle_body,
        out_shape=[jax.ShapeDtypeStruct(v.shape, v.dtype) for v in made],
        in_specs=[vmem] * 4,
        out_specs=[vmem] * 4,
        name="settle",
    )(*made)


def shards(tokens, attn_gain, q_gain, k_gain, ffn_gain, w_query, w_keyval, w_out, prior_cache, prior_len, stretch_len):
    made = block(
        tokens[0], attn_gain, q_gain, k_gain, ffn_gain, w_query, w_keyval, w_out.T, prior_cache, prior_len, stretch_len
    )
    return tuple(v[None] for v in settle(*made))


def solution(mesh):
    placed = (
        P("seq", None, None),
        P(),
        P(),
        P(),
        P(),
        P("seq", "head"),
        P("seq", None),
        P("head", "seq"),
        P(None, "seq", None),
        P(),
        P(),
    )
    return jax.shard_map(
        shards,
        mesh=mesh,
        in_specs=placed,
        out_specs=(P("seq", "head", None),) * 4,
        check_vma=False,
    )
```

```python
import math

import jax
import jax.numpy as jnp
from jax import lax
from jax.experimental import pallas as pl
from jax.experimental.pallas import tpu as pltpu
from jax.sharding import PartitionSpec as P

HD = 64
NX, NZ, NY = 4, 16, 4
PLANE = NZ * 2
A, B = 640, 256
MESH = pl.DeviceIdType.MESH
BF = jnp.bfloat16
F32 = jnp.float32
epsilon = 1e-06


def body(
    tok_in, again_in, qgain_in, kgain_in, fgain_in, wq_in, wkv_in, wo_in, cache_in, prior_in, stretch_in,
    hidden, ffn, fresh, decode,
    tok, again, qgain, kgain, fgain, wq, wkv, wo, cache, prior, stretch, i_sem,
    wa, wb, cpack, xb, eb, yb, normed, acc, qs, kvs, kvr, tb, rb, cosine, sine,
    a_send, a_recv, b_send, b_recv, x_send, x_recv, e_send, e_recv, y_send, y_recv, k_send, k_recv, t_send, t_recv,
):
    s = lax.axis_index("seq")
    h = lax.axis_index("head")
    x = s // PLANE
    low = lax.rem(s, PLANE)
    z = low // 2
    c = lax.rem(low, 2)

    def sid(xx, zz, cc):
        return xx * PLANE + zz * 2 + cc

    def wrapx(v):
        return lax.rem(v + NX, NX)

    def wrapz(v):
        return lax.rem(v + NZ, NZ)

    barrier = pltpu.get_barrier_semaphore()

    def signal(target):
        pl.semaphore_signal(barrier, inc=1, device_id=target, device_id_type=MESH)

    def greet(k, carry):
        signal({"seq": x * PLANE + lax.rem(low + k, PLANE)})
        return carry

    lax.fori_loop(1, PLANE, greet, 0)
    for k in range(1, NX):
        signal({"seq": sid(wrapx(x + k), z, c)})
    for k in range(1, NY):
        signal({"head": lax.rem(h + k, NY)})

    taken = [
        pltpu.make_async_copy(src, dst, i_sem.at[i])
        for i, (src, dst) in enumerate(
            ((wq_in, wq), (wkv_in, wkv), (wo_in, wo), (cache_in, cache), (prior_in, prior), (tok_in, tok),
             (again_in, again), (qgain_in, qgain), (kgain_in, kgain), (fgain_in, fgain), (stretch_in, stretch))
        )
    ]
    for copy in taken:
        copy.start()
    for copy in taken[:3]:
        copy.wait()
    own = pl.ds(pl.multiple_of(s * 16, 16), 16)
    for head in range(NY):

        @pl.when(h == head)
        def _(head=head):
            lo = 64 * head
            wa[own, 0:128] = wkv[:, lo : lo + 128]
            wa[own, 128:256] = wkv[:, 320 + lo : 448 + lo]

    wa[own, 256:640] = jnp.concatenate([wq[...], wo[:, 0:64]], axis=1)
    wb[own, :] = wo[:, 64:320]

    pl.semaphore_wait(barrier, PLANE - 1 + NX - 1 + NY - 1)

    ahead = jnp.where(c == 0, 1, -1)
    partner = {"seq": sid(x, z, 1 - c)}

    def tox(d):
        return {"seq": sid(wrapx(x + d), z, c)}

    def toz(d):
        return {"seq": sid(x, wrapz(z + d), c)}

    class Ring:
        def __init__(self, buf, send, recv):
            self.buf, self.send, self.recv, self.count = buf, send, recv, 0

        def rows(self, b):
            return self.buf.at[pl.ds(pl.multiple_of(b * 16, 16), 16)]

        def push(self, b, target):
            self.count += 1
            pltpu.make_async_remote_copy(
                src_ref=self.rows(b),
                dst_ref=self.rows(b),
                send_sem=self.send,
                recv_sem=self.recv.at[b],
                device_id=target,
                device_id_type=MESH,
            ).start()

        def arrive(self, b):
            pltpu.make_async_copy(self.rows(b), self.rows(b), self.recv.at[b]).wait()

        def spread(self, b):
            self.push(b, tox(ahead))
            self.push(b, tox(-ahead))
            self.push(b, partner)

        def near(self, b):
            for d in (2, -2, 1, -1):
                self.push(b, toz(d))

        def start(self):
            for d in (5, -5):
                self.push(s, toz(d))
            self.near(s)
            self.spread(s)

        def here(self, d, far=False):
            b = sid(x, wrapz(z + d), c)
            self.arrive(b)
            if far:
                self.near(b)
                if d == 5:
                    self.push(b, toz(-3))
            self.spread(b)

        def hop(self, d):
            b = sid(x, wrapz(z + d), c)
            self.arrive(b)
            self.near(b)
            if d == 5:
                self.push(b, toz(-3))

        def out(self, d):
            self.spread(sid(x, wrapz(z + d), c))

        def relay(self, d):
            b = sid(wrapx(x - ahead), wrapz(z + d), c)
            self.arrive(b)
            self.push(b, tox(ahead))
            self.push(b, partner)
            b = sid(wrapx(x + ahead), wrapz(z + d), c)
            self.arrive(b)
            self.push(b, partner)

        def last(self, d):
            b = sid(wrapx(x + 2), wrapz(z + d), c)
            self.arrive(b)
            self.push(b, partner)

        def shared(self, xx):
            def one(zz, carry):
                self.arrive(sid(xx, zz, 1 - c))
                return carry

            lax.fori_loop(0, NZ, one, 0)

        def drain(self):
            left = self.count
            while left > 0:
                n = min(left, 128)
                part = self.buf.at[pl.ds(0, n * 16)]
                pltpu.make_async_copy(part, part, self.send).wait()
                left -= n

    ra, rbq = Ring(wa, a_send, a_recv), Ring(wb, b_send, b_recv)
    ra.start()
    for copy in taken[3:]:
        copy.wait()
    for head in range(NY):

        @pl.when(h == head)
        def _(head=head):
            lo = 64 * head

            def pack(i, carry):
                at = pl.ds(pl.multiple_of(i * 16, 16), 16)
                cpack[at, :, 0:128] = cache[at, :, lo : lo + 128]
                cpack[at, :, 128:256] = cache[at, :, 320 + lo : 448 + lo]
                return carry

            lax.fori_loop(0, 8, pack, 0)

    prior_count = prior[s]
    pair_lane = lax.rem(lax.broadcasted_iota(jnp.int32, (128, 128), 1), 64)
    inverse = jnp.exp(lax.rem(pair_lane, 32).astype(F32) * (-2.0 * math.log(10000.0) / HD))
    angles = (prior_count + lax.broadcasted_iota(jnp.int32, (128, 128), 0)).astype(F32) * inverse
    cosine[...] = jnp.cos(angles)
    sines = jnp.sin(angles)
    sine[...] = jnp.where(pair_lane < 32, -sines, sines)
    for k in (2, 1, 3):
        xx = wrapx(x + k)
        pltpu.make_async_remote_copy(
            src_ref=cpack.at[pl.ds(pl.multiple_of(xx * PLANE, PLANE), PLANE)],
            dst_ref=xb.at[x],
            send_sem=x_send,
            recv_sem=x_recv,
            device_id=tox(k),
            device_id_type=MESH,
        ).start()
    pltpu.make_async_copy(cpack.at[pl.ds(pl.multiple_of(x * PLANE, PLANE), PLANE)], xb.at[x], x_recv).start()
    near, far = (1, -1, 2, -2), (5, -5)
    rest = (4, -4, 6, -6, 3, -3, 7, -7)
    rbq.start()
    def norm(i, carry):
        at = pl.ds(pl.multiple_of(i * 16, 16), 16)
        v = tok[at, :].astype(F32)
        v = v * lax.rsqrt(jnp.mean(v * v, axis=-1, keepdims=True) + epsilon) * again[...].astype(F32)[None, :]
        normed[at, :] = v.astype(BF)
        return carry

    lax.fori_loop(0, 8, norm, 0)
    for d in near:
        ra.here(d)
    ra.relay(0)
    for d in far:
        ra.here(d, True)
    for d in far:
        rbq.hop(d)
    pltpu.make_async_copy(xb, xb, x_recv).wait()

    def hand(k, carry):
        to = lax.rem(low + k, PLANE)
        pltpu.make_async_remote_copy(
            src_ref=xb.at[:, to],
            dst_ref=eb.at[:, low],
            send_sem=e_send,
            recv_sem=e_recv,
            device_id={"seq": x * PLANE + to},
            device_id_type=MESH,
        ).start()
        return carry

    lax.fori_loop(1, PLANE, hand, 0)
    pltpu.make_async_copy(xb.at[:, low], eb.at[:, low], e_recv).start()
    for d in near:
        ra.relay(d)
    ra.last(0)
    ra.here(8)
    for d in rest:
        ra.here(d)
    for d in far:
        ra.relay(d)
    for d in near:
        ra.last(d)
    for d in near:
        rbq.here(d)
    for d in far:
        rbq.out(d)
    ra.relay(8)
    for d in rest:
        ra.relay(d)
    for d in far:
        ra.last(d)
    rbq.relay(0)
    ra.shared(x)

    def project(xx, first=False):
        deep = pl.ds(pl.multiple_of(xx * 512, 512), 512)
        part = jnp.dot(normed[:, deep], wa[deep, :], preferred_element_type=F32)
        if first:
            acc[...] = part
        else:
            acc[...] += part

    project(x, True)
    ra.last(8)
    for d in rest:
        ra.last(d)
    rbq.here(8)
    for d in rest:
        rbq.here(d)
    ra.shared(wrapx(x + 1))
    project(wrapx(x + 1))
    ra.shared(wrapx(x - 1))
    project(wrapx(x - 1))
    for d in near:
        rbq.relay(d)
    rbq.last(0)
    for d in far:
        rbq.relay(d)
    for d in near:
        rbq.last(d)
    ra.shared(wrapx(x + 2))
    project(wrapx(x + 2))
    rbq.relay(8)
    for d in rest:
        rbq.relay(d)

    lane = lax.broadcasted_iota(jnp.int32, (128, 128), 1)
    row = lax.broadcasted_iota(jnp.int32, (128, 128), 0)
    upper = lane >= 64
    flip = lax.rem(lane, 64) < 32

    def position(t, gain):
        sq = t * t
        lo = jnp.sum(jnp.where(upper, 0.0, sq), axis=-1, keepdims=True)
        hi = jnp.sum(jnp.where(upper, sq, 0.0), axis=-1, keepdims=True)
        v = t * lax.rsqrt(jnp.where(upper, hi, lo) * (1.0 / 64) + epsilon) * gain
        turned = jnp.where(flip, pltpu.roll(v, 96, 1), pltpu.roll(v, 32, 1))
        return v * cosine[...] + turned * sine[...]

    def twice(gain):
        g = gain[...].astype(F32)[None, :]
        return jnp.concatenate([g, g], axis=1)

    keys = position(acc[:, 0:128], twice(kgain)).astype(BF)
    values = acc[:, 128:256].astype(BF)
    kvs[:, :, 0:128] = keys.reshape(NY, 32, 128)
    kvs[:, :, 128:256] = values.reshape(NY, 32, 128)
    kvr[h] = kvs[h]
    for k in (2, 1, 3):
        to = lax.rem(h + k, NY)
        pltpu.make_async_remote_copy(
            src_ref=kvs.at[to],
            dst_ref=kvr.at[h],
            send_sem=k_send,
            recv_sem=k_recv,
            device_id={"head": to},
            device_id_type=MESH,
        ).start()
    second = [jnp.where(i >= 4 - h, 1, 0) for i in range(5)]
    for pair in range(3):
        t = position(acc[:, 256 + 128 * pair : 384 + 128 * pair], twice(qgain))
        r = pltpu.roll(t, 64, 1)
        for half in range(2):
            i = 2 * pair + half
            if i < 5:
                v = jnp.where(second[i] == half, t, r)
                v = jnp.where(jnp.where(upper, 1, 0) == second[i], v, 0.0)
                qs[128 * i : 128 * (i + 1), :] = v.astype(BF)

    pltpu.make_async_copy(eb, eb, e_recv).wait()
    for k in (2, 1, 3):
        to = lax.rem(h + k, NY)
        pltpu.make_async_remote_copy(
            src_ref=eb.at[to],
            dst_ref=yb.at[h],
            send_sem=y_send,
            recv_sem=y_recv,
            device_id={"head": to},
            device_id_type=MESH,
        ).start()
    pltpu.make_async_copy(eb.at[h], yb.at[h], y_recv).start()
    stored = [eb[p].reshape(128, 256) for p in range(4)]
    all_keys = jnp.concatenate([t[:, 0:128] for t in stored] + [keys], axis=0)
    all_values = jnp.concatenate([t[:, 128:256] for t in stored] + [values], axis=0)
    slot = lax.broadcasted_iota(jnp.int32, (128, 512), 1)
    earlier = slot < prior_count
    causal = lane <= row
    allowed = jnp.concatenate([earlier, causal], axis=1)
    heads = []
    for i in range(5):
        sc = lax.dot_general(
            qs[128 * i : 128 * (i + 1), :], all_keys, (((1,), (1,)), ((), ())), preferred_element_type=F32
        ) * (1.0 / math.sqrt(HD))
        sc = jnp.where(allowed, sc, -jnp.inf)
        w = jnp.exp(sc - jnp.max(sc, axis=-1, keepdims=True))
        total = jnp.sum(w, axis=-1, keepdims=True)
        m = jnp.dot(w.astype(BF), all_values, preferred_element_type=F32) / total
        heads.append(jnp.where(second[i] == (i + 1) % 2, m, pltpu.roll(m, 64, 1)))
    att = [
        jnp.where(upper, heads[0], 0.0).astype(BF),
        jnp.where(upper, heads[2], heads[1]).astype(BF),
        jnp.where(upper, heads[4], heads[3]).astype(BF),
    ]
    att12 = jnp.concatenate(att[1:], axis=1)

    def project_out(xx):
        wide = pl.ds(pl.multiple_of(xx * 512, 512), 512)
        dims = (((1,), (1,)), ((), ()))
        part = lax.dot_general(att[0], wa[wide, 512:640], dims, preferred_element_type=F32)
        part = part + lax.dot_general(att12, wb[wide, :], dims, preferred_element_type=F32)
        tb[:, :, wide] = part.astype(BF).reshape(NY, 32, 512)
        for k in (2, 1, 3):
            to = lax.rem(h + k, NY)
            pltpu.make_async_remote_copy(
                src_ref=tb.at[to, :, wide],
                dst_ref=rb.at[h, :, wide],
                send_sem=t_send,
                recv_sem=t_recv,
                device_id={"head": to},
                device_id_type=MESH,
            ).start()

    rbq.shared(x)
    project_out(x)
    for d in far:
        rbq.last(d)
    rbq.shared(wrapx(x + 1))
    project_out(wrapx(x + 1))
    for d in (8,) + rest:
        rbq.last(d)
    for d in (-1, 2):
        rbq.shared(wrapx(x + d))
        project_out(wrapx(x + d))

    limit = stretch[s]

    def assemble(t0, t1, t2, t3):
        low_half = lax.broadcasted_iota(jnp.int32, (t0.shape[0], 128), 1) < 64
        mid = pltpu.roll(jnp.where(low_half, t0[:, 128:256].astype(F32), t3[:, 0:128].astype(F32)), 64, 1).astype(BF)
        return jnp.concatenate([t0[:, 0:128], t2[:, 0:128], mid, t1[:, 128:256], t3[:, 128:256]], axis=1)

    pltpu.make_async_copy(yb, yb, y_recv).wait()
    decode[...] = assemble(*[yb[p].reshape(128, 256) for p in range(4)])
    three = kvr.at[pl.ds(0, 3)]
    pltpu.make_async_copy(three, three, k_recv).wait()
    rows = h * 32 + lax.broadcasted_iota(jnp.int32, (32, 640), 0)
    made = assemble(*[kvr[p] for p in range(4)])
    fresh[...] = jnp.where(rows < limit, made, jnp.zeros_like(made))

    three = rb.at[pl.ds(0, 3)]
    pltpu.make_async_copy(three, three, t_recv).wait()
    summed = tok[pl.ds(pl.multiple_of(h * 32, 32), 32), :].astype(F32)
    share = tb[h].astype(F32)
    for k in range(1, NY):
        share = share + rb[lax.rem(h + k, NY)].astype(F32)
    resid = summed + share
    valid = h * 32 + lax.broadcasted_iota(jnp.int32, (32, 2048), 0) < limit
    hidden[...] = jnp.where(valid, resid, 0.0).astype(BF)
    scaled = resid * lax.rsqrt(jnp.mean(resid * resid, axis=-1, keepdims=True) + epsilon) * fgain[...].astype(F32)[None, :]
    ffn[...] = jnp.where(valid, scaled, 0.0).astype(BF)

    for ref, sem in ((xb.at[pl.ds(0, 3)], x_send), (eb.at[:, pl.ds(0, PLANE - 1)], e_send),
                     (yb.at[pl.ds(0, 3)], y_send), (kvr.at[pl.ds(0, 3)], k_send), (rb.at[pl.ds(0, 3)], t_send)):
        pltpu.make_async_copy(ref, ref, sem).wait()
    ra.drain()
    rbq.drain()


def block(*args):
    vmem = pl.BlockSpec(memory_space=pltpu.VMEM)
    dma = pltpu.SemaphoreType.DMA
    many = pltpu.SemaphoreType.DMA((NX * PLANE,))
    cache_like = pltpu.VMEM((NX, PLANE, 4, 256), BF)
    return pl.pallas_call(
        body,
        out_shape=(
            jax.ShapeDtypeStruct((32, 2048), BF),
            jax.ShapeDtypeStruct((32, 2048), BF),
            jax.ShapeDtypeStruct((32, 640), BF),
            jax.ShapeDtypeStruct((128, 640), BF),
        ),
        in_specs=[pl.BlockSpec(memory_space=pltpu.HBM)] * 11,
        out_specs=(vmem,) * 4,
        scratch_shapes=[
            pltpu.VMEM((128, 2048), BF),
            pltpu.VMEM((2048,), BF),
            pltpu.VMEM((HD,), BF),
            pltpu.VMEM((HD,), BF),
            pltpu.VMEM((2048,), BF),
            pltpu.VMEM((16, 320), BF),
            pltpu.VMEM((16, 640), BF),
            pltpu.VMEM((16, 320), BF),
            pltpu.VMEM((128, 4, 640), BF),
            pltpu.SMEM((128,), jnp.int32),
            pltpu.SMEM((128,), jnp.int32),
            pltpu.SemaphoreType.DMA((11,)),
            pltpu.VMEM((2048, A), BF),
            pltpu.VMEM((2048, B), BF),
            pltpu.VMEM((128, 4, 256), BF),
            cache_like,
            cache_like,
            cache_like,
            pltpu.VMEM((128, 2048), BF),
            pltpu.VMEM((128, A), F32),
            pltpu.VMEM((640, 128), BF),
            pltpu.VMEM((NY, 32, 256), BF),
            pltpu.VMEM((NY, 32, 256), BF),
            pltpu.VMEM((NY, 32, 2048), BF),
            pltpu.VMEM((NY, 32, 2048), BF),
            pltpu.VMEM((128, 128), F32),
            pltpu.VMEM((128, 128), F32),
            dma, many, dma, many, dma, dma, dma, dma, dma, dma, dma, dma, dma, dma,
        ],
        compiler_params=pltpu.CompilerParams(collective_id=0, has_side_effects=True),
        name="block",
    )(*args)


def settle_body(*refs):
    for src, dst in zip(refs[:4], refs[4:]):
        dst[...] = src[...]


def settle(*made):
    vmem = pl.BlockSpec(memory_space=pltpu.VMEM)
    return pl.pallas_call(
        settle_body,
        out_shape=[jax.ShapeDtypeStruct(v.shape, v.dtype) for v in made],
        in_specs=[vmem] * 4,
        out_specs=[vmem] * 4,
        name="settle",
    )(*made)


def shards(tokens, attn_gain, q_gain, k_gain, ffn_gain, w_query, w_keyval, w_out, prior_cache, prior_len, stretch_len):
    made = block(
        tokens[0], attn_gain, q_gain, k_gain, ffn_gain, w_query, w_keyval, w_out.T, prior_cache, prior_len, stretch_len
    )
    return tuple(v[None] for v in settle(*made))


def solution(mesh):
    placed = (
        P("seq", None, None),
        P(),
        P(),
        P(),
        P(),
        P("seq", "head"),
        P("seq", None),
        P("head", "seq"),
        P(None, "seq", None),
        P(),
        P(),
    )
    return jax.shard_map(
        shards,
        mesh=mesh,
        in_specs=placed,
        out_specs=(P("seq", "head", None),) * 4,
        check_vma=False,
    )
```

```python
import math

import jax
import jax.numpy as jnp
from jax import lax
from jax.experimental import pallas as pl
from jax.experimental.pallas import tpu as pltpu
from jax.sharding import PartitionSpec as P

HD = 64
NX, NZ, NY = 4, 16, 4
PLANE = NZ * 2
A, B = 640, 256
MESH = pl.DeviceIdType.MESH
BF = jnp.bfloat16
F32 = jnp.float32
epsilon = 1e-06


def body(
    tok_in, again_in, qgain_in, kgain_in, fgain_in, wq_in, wkv_in, wo_in, cache_in, prior_in, stretch_in,
    hidden, ffn, fresh, decode,
    tok, again, qgain, kgain, fgain, wq, wkv, wo, cache, prior, stretch, i_sem,
    wa, wb, cpack, xb, eb, yb, normed, acc, qs, kvs, kvr, tb, rb, cosine, sine,
    a_send, a_recv, b_send, b_recv, x_send, x_recv, e_send, e_recv, y_send, y_recv, k_send, k_recv, t_send, t_recv,
):
    s = lax.axis_index("seq")
    h = lax.axis_index("head")
    x = s // PLANE
    low = lax.rem(s, PLANE)
    z = low // 2
    c = lax.rem(low, 2)

    def sid(xx, zz, cc):
        return xx * PLANE + zz * 2 + cc

    def wrapx(v):
        return lax.rem(v + NX, NX)

    def wrapz(v):
        return lax.rem(v + NZ, NZ)

    barrier = pltpu.get_barrier_semaphore()

    def signal(target):
        pl.semaphore_signal(barrier, inc=1, device_id=target, device_id_type=MESH)

    def greet(k, carry):
        signal({"seq": x * PLANE + lax.rem(low + k, PLANE)})
        return carry

    lax.fori_loop(1, PLANE, greet, 0)
    for k in range(1, NX):
        signal({"seq": sid(wrapx(x + k), z, c)})
    for k in range(1, NY):
        signal({"head": lax.rem(h + k, NY)})

    taken = [
        pltpu.make_async_copy(src, dst, i_sem.at[i])
        for i, (src, dst) in enumerate(
            ((wq_in, wq), (wkv_in, wkv), (wo_in, wo), (cache_in, cache), (prior_in, prior), (tok_in, tok),
             (again_in, again), (qgain_in, qgain), (kgain_in, kgain), (fgain_in, fgain), (stretch_in, stretch))
        )
    ]
    for copy in taken:
        copy.start()
    for copy in taken[:3]:
        copy.wait()
    own = pl.ds(pl.multiple_of(s * 16, 16), 16)
    for head in range(NY):

        @pl.when(h == head)
        def _(head=head):
            lo = 64 * head
            wa[own, 0:128] = wkv[:, lo : lo + 128]
            wa[own, 128:256] = wkv[:, 320 + lo : 448 + lo]

    wa[own, 256:640] = jnp.concatenate([wq[...], wo[:, 0:64]], axis=1)
    wb[own, :] = wo[:, 64:320]

    pl.semaphore_wait(barrier, PLANE - 1 + NX - 1 + NY - 1)

    ahead = jnp.where(c == 0, 1, -1)
    partner = {"seq": sid(x, z, 1 - c)}

    def tox(d):
        return {"seq": sid(wrapx(x + d), z, c)}

    def toz(d):
        return {"seq": sid(x, wrapz(z + d), c)}

    class Ring:
        def __init__(self, buf, send, recv):
            self.buf, self.send, self.recv, self.count = buf, send, recv, 0

        def rows(self, b):
            return self.buf.at[pl.ds(pl.multiple_of(b * 16, 16), 16)]

        def push(self, b, target):
            self.count += 1
            pltpu.make_async_remote_copy(
                src_ref=self.rows(b),
                dst_ref=self.rows(b),
                send_sem=self.send,
                recv_sem=self.recv.at[b],
                device_id=target,
                device_id_type=MESH,
            ).start()

        def arrive(self, b):
            pltpu.make_async_copy(self.rows(b), self.rows(b), self.recv.at[b]).wait()

        def spread(self, b):
            self.push(b, tox(ahead))
            self.push(b, tox(-ahead))
            self.push(b, partner)

        def near(self, b):
            for d in (2, -2, 1, -1):
                self.push(b, toz(d))

        def start(self):
            for d in (5, -5):
                self.push(s, toz(d))
            self.near(s)
            self.spread(s)

        def here(self, d, far=False):
            b = sid(x, wrapz(z + d), c)
            self.arrive(b)
            if far:
                self.near(b)
                if d == 5:
                    self.push(b, toz(-3))
            self.spread(b)

        def hop(self, d):
            b = sid(x, wrapz(z + d), c)
            self.arrive(b)
            self.near(b)
            if d == 5:
                self.push(b, toz(-3))

        def out(self, d):
            self.spread(sid(x, wrapz(z + d), c))

        def relay(self, d):
            b = sid(wrapx(x - ahead), wrapz(z + d), c)
            self.arrive(b)
            self.push(b, tox(ahead))
            self.push(b, partner)
            b = sid(wrapx(x + ahead), wrapz(z + d), c)
            self.arrive(b)
            self.push(b, partner)

        def last(self, d):
            b = sid(wrapx(x + 2), wrapz(z + d), c)
            self.arrive(b)
            self.push(b, partner)

        def shared(self, xx):
            def one(zz, carry):
                self.arrive(sid(xx, zz, 1 - c))
                return carry

            lax.fori_loop(0, NZ, one, 0)

        def drain(self):
            left = self.count
            while left > 0:
                n = min(left, 128)
                part = self.buf.at[pl.ds(0, n * 16)]
                pltpu.make_async_copy(part, part, self.send).wait()
                left -= n

    ra, rbq = Ring(wa, a_send, a_recv), Ring(wb, b_send, b_recv)
    ra.start()
    for copy in taken[3:]:
        copy.wait()
    for head in range(NY):

        @pl.when(h == head)
        def _(head=head):
            lo = 64 * head

            def pack(i, carry):
                at = pl.ds(pl.multiple_of(i * 16, 16), 16)
                cpack[at, :, 0:128] = cache[at, :, lo : lo + 128]
                cpack[at, :, 128:256] = cache[at, :, 320 + lo : 448 + lo]
                return carry

            lax.fori_loop(0, 8, pack, 0)

    prior_count = prior[s]
    pair_lane = lax.rem(lax.broadcasted_iota(jnp.int32, (128, 128), 1), 64)
    inverse = jnp.exp(lax.rem(pair_lane, 32).astype(F32) * (-2.0 * math.log(10000.0) / HD))
    angles = (prior_count + lax.broadcasted_iota(jnp.int32, (128, 128), 0)).astype(F32) * inverse
    cosine[...] = jnp.cos(angles)
    sines = jnp.sin(angles)
    sine[...] = jnp.where(pair_lane < 32, -sines, sines)
    for k in (2, 1, 3):
        xx = wrapx(x + k)
        pltpu.make_async_remote_copy(
            src_ref=cpack.at[pl.ds(pl.multiple_of(xx * PLANE, PLANE), PLANE)],
            dst_ref=xb.at[x],
            send_sem=x_send,
            recv_sem=x_recv,
            device_id=tox(k),
            device_id_type=MESH,
        ).start()
    pltpu.make_async_copy(cpack.at[pl.ds(pl.multiple_of(x * PLANE, PLANE), PLANE)], xb.at[x], x_recv).start()
    near, far = (1, -1, 2, -2), (5, -5)
    rest = (3, 7, 4, 6, -7, -3, -6, -4, 8)
    rbq.start()
    def norm(i, carry):
        at = pl.ds(pl.multiple_of(i * 16, 16), 16)
        v = tok[at, :].astype(F32)
        v = v * lax.rsqrt(jnp.mean(v * v, axis=-1, keepdims=True) + epsilon) * again[...].astype(F32)[None, :]
        normed[at, :] = v.astype(BF)
        return carry

    lax.fori_loop(0, 8, norm, 0)
    for d in near:
        ra.here(d)
    ra.relay(0)
    for d in far:
        ra.here(d, True)
    for d in far:
        rbq.hop(d)
    for d in near:
        ra.relay(d)
    ra.last(0)
    for d in rest:
        ra.here(d)
    pltpu.make_async_copy(xb, xb, x_recv).wait()

    def hand(k, carry):
        to = lax.rem(low + k, PLANE)
        pltpu.make_async_remote_copy(
            src_ref=xb.at[:, to],
            dst_ref=eb.at[:, low],
            send_sem=e_send,
            recv_sem=e_recv,
            device_id={"seq": x * PLANE + to},
            device_id_type=MESH,
        ).start()
        return carry

    lax.fori_loop(1, PLANE, hand, 0)
    pltpu.make_async_copy(xb.at[:, low], eb.at[:, low], e_recv).start()
    for d in far:
        ra.relay(d)
    for d in near:
        ra.last(d)
    for d in near:
        rbq.here(d)
    for d in far:
        rbq.out(d)
    for d in rest:
        ra.relay(d)
    for d in far:
        ra.last(d)
    rbq.relay(0)
    ra.shared(x)

    def project(xx, first=False):
        deep = pl.ds(pl.multiple_of(xx * 512, 512), 512)
        part = jnp.dot(normed[:, deep], wa[deep, :], preferred_element_type=F32)
        if first:
            acc[...] = part
        else:
            acc[...] += part

    project(x, True)
    for d in rest:
        ra.last(d)
    for d in rest:
        rbq.here(d)
    ra.shared(wrapx(x + 1))
    project(wrapx(x + 1))
    ra.shared(wrapx(x - 1))
    project(wrapx(x - 1))
    for d in near:
        rbq.relay(d)
    rbq.last(0)
    for d in far:
        rbq.relay(d)
    for d in near:
        rbq.last(d)
    ra.shared(wrapx(x + 2))
    project(wrapx(x + 2))
    for d in rest:
        rbq.relay(d)

    lane = lax.broadcasted_iota(jnp.int32, (128, 128), 1)
    row = lax.broadcasted_iota(jnp.int32, (128, 128), 0)
    upper = lane >= 64
    flip = lax.rem(lane, 64) < 32

    def position(t, gain):
        sq = t * t
        lo = jnp.sum(jnp.where(upper, 0.0, sq), axis=-1, keepdims=True)
        hi = jnp.sum(jnp.where(upper, sq, 0.0), axis=-1, keepdims=True)
        v = t * lax.rsqrt(jnp.where(upper, hi, lo) * (1.0 / 64) + epsilon) * gain
        turned = jnp.where(flip, pltpu.roll(v, 96, 1), pltpu.roll(v, 32, 1))
        return v * cosine[...] + turned * sine[...]

    def twice(gain):
        g = gain[...].astype(F32)[None, :]
        return jnp.concatenate([g, g], axis=1)

    keys = position(acc[:, 0:128], twice(kgain)).astype(BF)
    values = acc[:, 128:256].astype(BF)
    kvs[:, :, 0:128] = keys.reshape(NY, 32, 128)
    kvs[:, :, 128:256] = values.reshape(NY, 32, 128)
    kvr[h] = kvs[h]
    for k in (2, 1, 3):
        to = lax.rem(h + k, NY)
        pltpu.make_async_remote_copy(
            src_ref=kvs.at[to],
            dst_ref=kvr.at[h],
            send_sem=k_send,
            recv_sem=k_recv,
            device_id={"head": to},
            device_id_type=MESH,
        ).start()
    second = [jnp.where(i >= 4 - h, 1, 0) for i in range(5)]
    for pair in range(3):
        t = position(acc[:, 256 + 128 * pair : 384 + 128 * pair], twice(qgain))
        r = pltpu.roll(t, 64, 1)
        for half in range(2):
            i = 2 * pair + half
            if i < 5:
                v = jnp.where(second[i] == half, t, r)
                v = jnp.where(jnp.where(upper, 1, 0) == second[i], v, 0.0)
                qs[128 * i : 128 * (i + 1), :] = v.astype(BF)

    pltpu.make_async_copy(eb, eb, e_recv).wait()
    for k in (2, 1, 3):
        to = lax.rem(h + k, NY)
        pltpu.make_async_remote_copy(
            src_ref=eb.at[to],
            dst_ref=yb.at[h],
            send_sem=y_send,
            recv_sem=y_recv,
            device_id={"head": to},
            device_id_type=MESH,
        ).start()
    pltpu.make_async_copy(eb.at[h], yb.at[h], y_recv).start()
    stored = [eb[p].reshape(128, 256) for p in range(4)]
    all_keys = jnp.concatenate([t[:, 0:128] for t in stored] + [keys], axis=0)
    all_values = jnp.concatenate([t[:, 128:256] for t in stored] + [values], axis=0)
    slot = lax.broadcasted_iota(jnp.int32, (128, 512), 1)
    earlier = slot < prior_count
    causal = lane <= row
    allowed = jnp.concatenate([earlier, causal], axis=1)
    heads = []
    for i in range(5):
        sc = lax.dot_general(
            qs[128 * i : 128 * (i + 1), :], all_keys, (((1,), (1,)), ((), ())), preferred_element_type=F32
        ) * (1.0 / math.sqrt(HD))
        sc = jnp.where(allowed, sc, -jnp.inf)
        w = jnp.exp(sc - jnp.max(sc, axis=-1, keepdims=True))
        total = jnp.sum(w, axis=-1, keepdims=True)
        m = jnp.dot(w.astype(BF), all_values, preferred_element_type=F32) / total
        heads.append(jnp.where(second[i] == (i + 1) % 2, m, pltpu.roll(m, 64, 1)))
    att = [
        jnp.where(upper, heads[0], 0.0).astype(BF),
        jnp.where(upper, heads[2], heads[1]).astype(BF),
        jnp.where(upper, heads[4], heads[3]).astype(BF),
    ]
    att12 = jnp.concatenate(att[1:], axis=1)

    def project_out(xx):
        wide = pl.ds(pl.multiple_of(xx * 512, 512), 512)
        dims = (((1,), (1,)), ((), ()))
        part = lax.dot_general(att[0], wa[wide, 512:640], dims, preferred_element_type=F32)
        part = part + lax.dot_general(att12, wb[wide, :], dims, preferred_element_type=F32)
        tb[:, :, wide] = part.astype(BF).reshape(NY, 32, 512)
        for k in (2, 1, 3):
            to = lax.rem(h + k, NY)
            pltpu.make_async_remote_copy(
                src_ref=tb.at[to, :, wide],
                dst_ref=rb.at[h, :, wide],
                send_sem=t_send,
                recv_sem=t_recv,
                device_id={"head": to},
                device_id_type=MESH,
            ).start()

    rbq.shared(x)
    project_out(x)
    for d in far:
        rbq.last(d)
    rbq.shared(wrapx(x + 1))
    project_out(wrapx(x + 1))
    for d in rest:
        rbq.last(d)
    for d in (-1, 2):
        rbq.shared(wrapx(x + d))
        project_out(wrapx(x + d))

    limit = stretch[s]

    def assemble(t0, t1, t2, t3):
        low_half = lax.broadcasted_iota(jnp.int32, (t0.shape[0], 128), 1) < 64
        mid = pltpu.roll(jnp.where(low_half, t0[:, 128:256].astype(F32), t3[:, 0:128].astype(F32)), 64, 1).astype(BF)
        return jnp.concatenate([t0[:, 0:128], t2[:, 0:128], mid, t1[:, 128:256], t3[:, 128:256]], axis=1)

    pltpu.make_async_copy(yb, yb, y_recv).wait()
    decode[...] = assemble(*[yb[p].reshape(128, 256) for p in range(4)])
    three = kvr.at[pl.ds(0, 3)]
    pltpu.make_async_copy(three, three, k_recv).wait()
    rows = h * 32 + lax.broadcasted_iota(jnp.int32, (32, 640), 0)
    made = assemble(*[kvr[p] for p in range(4)])
    fresh[...] = jnp.where(rows < limit, made, jnp.zeros_like(made))

    three = rb.at[pl.ds(0, 3)]
    pltpu.make_async_copy(three, three, t_recv).wait()
    summed = tok[pl.ds(pl.multiple_of(h * 32, 32), 32), :].astype(F32)
    share = tb[h].astype(F32)
    for k in range(1, NY):
        share = share + rb[lax.rem(h + k, NY)].astype(F32)
    resid = summed + share
    valid = h * 32 + lax.broadcasted_iota(jnp.int32, (32, 2048), 0) < limit
    hidden[...] = jnp.where(valid, resid, 0.0).astype(BF)
    scaled = resid * lax.rsqrt(jnp.mean(resid * resid, axis=-1, keepdims=True) + epsilon) * fgain[...].astype(F32)[None, :]
    ffn[...] = jnp.where(valid, scaled, 0.0).astype(BF)

    for ref, sem in ((xb.at[pl.ds(0, 3)], x_send), (eb.at[:, pl.ds(0, PLANE - 1)], e_send),
                     (yb.at[pl.ds(0, 3)], y_send), (kvr.at[pl.ds(0, 3)], k_send), (rb.at[pl.ds(0, 3)], t_send)):
        pltpu.make_async_copy(ref, ref, sem).wait()
    ra.drain()
    rbq.drain()


def block(*args):
    vmem = pl.BlockSpec(memory_space=pltpu.VMEM)
    dma = pltpu.SemaphoreType.DMA
    many = pltpu.SemaphoreType.DMA((NX * PLANE,))
    cache_like = pltpu.VMEM((NX, PLANE, 4, 256), BF)
    return pl.pallas_call(
        body,
        out_shape=(
            jax.ShapeDtypeStruct((32, 2048), BF),
            jax.ShapeDtypeStruct((32, 2048), BF),
            jax.ShapeDtypeStruct((32, 640), BF),
            jax.ShapeDtypeStruct((128, 640), BF),
        ),
        in_specs=[pl.BlockSpec(memory_space=pltpu.HBM)] * 11,
        out_specs=(vmem,) * 4,
        scratch_shapes=[
            pltpu.VMEM((128, 2048), BF),
            pltpu.VMEM((2048,), BF),
            pltpu.VMEM((HD,), BF),
            pltpu.VMEM((HD,), BF),
            pltpu.VMEM((2048,), BF),
            pltpu.VMEM((16, 320), BF),
            pltpu.VMEM((16, 640), BF),
            pltpu.VMEM((16, 320), BF),
            pltpu.VMEM((128, 4, 640), BF),
            pltpu.SMEM((128,), jnp.int32),
            pltpu.SMEM((128,), jnp.int32),
            pltpu.SemaphoreType.DMA((11,)),
            pltpu.VMEM((2048, A), BF),
            pltpu.VMEM((2048, B), BF),
            pltpu.VMEM((128, 4, 256), BF),
            cache_like,
            cache_like,
            cache_like,
            pltpu.VMEM((128, 2048), BF),
            pltpu.VMEM((128, A), F32),
            pltpu.VMEM((640, 128), BF),
            pltpu.VMEM((NY, 32, 256), BF),
            pltpu.VMEM((NY, 32, 256), BF),
            pltpu.VMEM((NY, 32, 2048), BF),
            pltpu.VMEM((NY, 32, 2048), BF),
            pltpu.VMEM((128, 128), F32),
            pltpu.VMEM((128, 128), F32),
            dma, many, dma, many, dma, dma, dma, dma, dma, dma, dma, dma, dma, dma,
        ],
        compiler_params=pltpu.CompilerParams(collective_id=0, has_side_effects=True),
        name="block",
    )(*args)


def settle_body(*refs):
    made, out, held, into, onto = refs[:4], refs[4:8], refs[8:12], refs[12], refs[13]
    first = [pltpu.make_async_copy(made[i], held[i], into.at[i]) for i in range(4)]
    then = [pltpu.make_async_copy(held[i], out[i], onto.at[i]) for i in range(4)]
    for copy in first:
        copy.start()
    for i in range(4):
        first[i].wait()
        then[i].start()
    for copy in then:
        copy.wait()


def settle(*made):
    hbm = pl.BlockSpec(memory_space=pltpu.HBM)
    return pl.pallas_call(
        settle_body,
        out_shape=[jax.ShapeDtypeStruct(v.shape, v.dtype) for v in made],
        in_specs=[hbm] * 4,
        out_specs=[hbm] * 4,
        scratch_shapes=[pltpu.VMEM(v.shape, v.dtype) for v in made] + [pltpu.SemaphoreType.DMA((4,))] * 2,
        name="settle",
    )(*made)


def shards(tokens, attn_gain, q_gain, k_gain, ffn_gain, w_query, w_keyval, w_out, prior_cache, prior_len, stretch_len):
    made = block(
        tokens[0], attn_gain, q_gain, k_gain, ffn_gain, w_query, w_keyval, w_out.T, prior_cache, prior_len, stretch_len
    )
    return tuple(v[None] for v in settle(*made))


def solution(mesh):
    placed = (
        P("seq", None, None),
        P(),
        P(),
        P(),
        P(),
        P("seq", "head"),
        P("seq", None),
        P("head", "seq"),
        P(None, "seq", None),
        P(),
        P(),
    )
    return jax.shard_map(
        shards,
        mesh=mesh,
        in_specs=placed,
        out_specs=(P("seq", "head", None),) * 4,
        check_vma=False,
    )
```
